32 devices in a mesh: fsdp: 4 (over y, x), ctx: 8 (over z, core).
Axes of the slice: x: 2, y: 2, z: 4, core: 2. Of those that a mesh axis runs over, the one named last changes fastest.
Arguments:
- block_input: bfloat16 [8, 512, 1088], P('fsdp', 'ctx'), may hold values from -6 to 6
- positions: int32 [8, 512], P('fsdp', 'ctx'), may hold values from 0 to 511, as said below
- prefix: int32 [8], P('fsdp'), may hold values from 0 to 255
- first_gain: float32 [1088], replicated, may hold values from 0.25 to 1.75
- first_bias: float32 [1088], replicated, may hold values from -3 to 3
- query_key_value: bfloat16 [1088, 3264], P('fsdp')
- query_value_bias: float32 [2, 1088], replicated, may hold values from -3 to 3
- output_weight: bfloat16 [1088, 1088], P('fsdp'), may hold values from -1.5 to 1.5
- output_bias: float32 [1088], replicated, may hold values from -3 to 3
- second_gain: float32 [1088], replicated, may hold values from 0.25 to 1.75
- second_bias: float32 [1088], replicated, may hold values from -3 to 3
- expand_weight: bfloat16 [1088, 4352], P('fsdp'), may hold values from -0.1875 to 0.1875
- expand_bias: float32 [4352], replicated, may hold values from -3 to 3
- contract_weight: bfloat16 [4352, 1088], P('fsdp'), may hold values from -0.09375 to 0.09375
- contract_bias: float32 [1088], replicated, may hold values from -3 to 3
- cotangent: bfloat16 [8, 512, 1088], P('fsdp', 'ctx'), may hold values from -6 to 6
Outputs:
- block_output: bfloat16 [8, 512, 1088], P('fsdp', 'ctx')
- input_gradient: float32 [8, 512, 1088], P('fsdp', 'ctx')
- first_gain_gradient: float32 [1088], replicated
- first_bias_gradient: float32 [1088], replicated
- query_key_value_gradient: float32 [1088, 3264], P('fsdp')
- query_value_bias_gradient: float32 [2, 1088], replicated
- output_weight_gradient: float32 [1088, 1088], P('fsdp')
- output_bias_gradient: float32 [1088], replicated
- second_gain_gradient: float32 [1088], replicated
- second_bias_gradient: float32 [1088], replicated
- expand_weight_gradient: float32 [1088, 4352], P('fsdp')
- expand_bias_gradient: float32 [4352], replicated
- contract_weight_gradient: float32 [4352, 1088], P('fsdp')
- contract_bias_gradient: float32 [1088], replicated
The draws below stay inside these ranges and needn't reach their ends.
Inputs may be any that keep to these rules, and one draw needn't show every extreme that they name: Each row lists the positions 0 to 511 once, as blocks of 64 consecutive increasing positions whose order along the row is arbitrary; a device's tokens of a sequence form one such block.
All inputs are finite; a program needn't handle non-finite values.
Results may differ from the reference program's by a relative error of at most 0.017.
Values may be sent and summed in bfloat16 or wider, within the bound.
No kernel may reach another device: no remote copies, remote signals or barrier semaphores. Data moves between devices by JAX's collectives and lax.ppermute only.
A program may use at most 256 MiB of HBM per device.

```python
import jax
import jax.numpy as jnp
from jax import lax

D = 1088
HEADS = 17
HEAD_DIM = 64
FF = 4352
PIECE = 64
SEQS = 8
LENGTH = 512


def draw_positions(key, part):
    blocks = LENGTH // PIECE
    seq_keys = jax.random.split(key, SEQS)
    orders = jax.vmap(lambda single: jax.random.permutation(single, blocks))(seq_keys).astype(jnp.int32)
    offsets = jnp.arange(PIECE, dtype=jnp.int32)
    return (orders[:, :, None] * PIECE + offsets[None, None, :]).reshape(SEQS, LENGTH)


def draw_query_key_value(key, part):
    base = jax.random.normal(jax.random.fold_in(key, 11), (D, 3 * D), jnp.float32) * D ** (-0.5)
    return base.astype(jnp.bfloat16)


def plant(values, stream_key, smallest, largest):
    dims = values.shape
    place = [jax.random.randint(jax.random.fold_in(stream_key, axis), (), 0, dims[axis]) for axis in range(len(dims))]
    values = values.at[tuple(place)].set(smallest)
    longest = dims.index(max(dims))
    place[longest] = (place[longest] + 1) % dims[longest]
    return values.at[tuple(place)].set(largest)


def level_of(own_key, extent, shards, least, high):
    level = 1.0
    for dim, parts in shards:
        steps = jax.random.uniform(jax.random.fold_in(jax.random.fold_in(own_key, 6), dim), (parts,), jnp.float32, least / len(shards), high / len(shards))
        level = level * jnp.repeat(jnp.exp(steps), extent[dim] // parts).reshape((-1,) + (1,) * (len(extent) - 1 - dim))
    return level


def normal_values(rng, shape, scale, most, pieces=(), held_as=jnp.bfloat16):
    values = scale * jax.random.normal(rng, shape, jnp.float32)
    if pieces:
        values = values * level_of(rng, shape, pieces, -0.22, 0.18)
    return jnp.clip(values, -most, most).astype(held_as)


def setup_inputs(seed: int = 0) -> dict:
    arg_keys = jax.random.split(jax.random.key(seed), 17)
    return {
        "block_input": normal_values(arg_keys[0], (SEQS, LENGTH, D), 1.0, 6.0, ((0, 4), (1, 8))),
        "positions": draw_positions(jax.random.fold_in(arg_keys[16], 71), 0),
        "prefix": plant(jax.random.randint(arg_keys[2], (SEQS,), 0, LENGTH // 2), jax.random.fold_in(arg_keys[2], 1), 0, (LENGTH // 2) - 1).astype(jnp.int32),
        "first_gain": jnp.clip(1.0 + 0.15 * jax.random.normal(arg_keys[3], (D,), jnp.float32), 0.25, 1.75),
        "first_bias": normal_values(arg_keys[4], (D,), 0.5, 3.0, (), jnp.float32),
        "query_key_value": draw_query_key_value(jax.random.fold_in(arg_keys[16], 71), 0),
        "query_value_bias": normal_values(arg_keys[6], (2, D), 0.5, 3.0, (), jnp.float32),
        "output_weight": normal_values(arg_keys[7], (D, D), (max(D // 64, 1)) ** -0.5, 1.5, ((0, 4),)),
        "output_bias": normal_values(arg_keys[8], (D,), 0.5, 3.0, (), jnp.float32),
        "second_gain": jnp.clip(1.0 + 0.15 * jax.random.normal(arg_keys[9], (D,), jnp.float32), 0.25, 1.75),
        "second_bias": normal_values(arg_keys[10], (D,), 0.5, 3.0, (), jnp.float32),
        "expand_weight": normal_values(arg_keys[11], (D, FF), D ** -0.5, 0.1875, ((0, 4),)),
        "expand_bias": normal_values(arg_keys[12], (FF,), 0.5, 3.0, (), jnp.float32),
        "contract_weight": normal_values(arg_keys[13], (FF, D), FF ** -0.5, 0.09375, ((0, 4),)),
        "contract_bias": normal_values(arg_keys[14], (D,), 0.5, 3.0, (), jnp.float32),
        "cotangent": normal_values(arg_keys[15], (SEQS, LENGTH, D), 1.0, 6.0, ((0, 4), (1, 8))),
    }


EPSILON = 1e-05
NEGATIVE = -1e+30

def layer_norm(values, gain, bias):
    center = values - lax.optimization_barrier(jnp.mean(values, axis=-1, keepdims=True))
    inverse = lax.rsqrt(lax.optimization_barrier(jnp.mean(center * center, axis=-1, keepdims=True)) + EPSILON)
    normed = center * inverse
    return (normed * gain + bias, normed, inverse)

def norm_back(upper, normed, inverse, gain):
    scaled = upper * gain
    return inverse * (scaled - lax.optimization_barrier(jnp.mean(scaled, axis=-1, keepdims=True)) - normed * lax.optimization_barrier(jnp.mean(scaled * normed, axis=-1, keepdims=True)))

def rounded(values):
    return lax.optimization_barrier(values.astype(jnp.bfloat16)).astype(jnp.float32)

def gelu(values):
    return jax.nn.gelu(values, approximate=True)

def attend(query, keys, values, places, start_prefix):
    scale = HEAD_DIM ** (-0.5)
    span = min(512, LENGTH)
    query_heads = query.astype(jnp.float32).reshape(LENGTH, HEADS, HEAD_DIM)
    key_heads = keys.astype(jnp.float32).reshape(LENGTH, HEADS, HEAD_DIM)
    value_heads = values.astype(jnp.float32).reshape(LENGTH, HEADS, HEAD_DIM)
    limits = jnp.maximum(places, start_prefix - 1)

    def one_block(number):
        start = number * span
        part = lax.dynamic_slice_in_dim(query_heads, start, span, 0)
        limit = lax.dynamic_slice_in_dim(limits, start, span, 0)
        scores = jnp.einsum('qhd,khd->hqk', part, key_heads) * scale
        visible = places[None, None, :] <= limit[None, :, None]
        scores = jnp.where(visible, scores, NEGATIVE)
        top = lax.optimization_barrier(jnp.max(scores, axis=-1, keepdims=True))
        log_total = top + jnp.log(lax.optimization_barrier(jnp.sum(jnp.exp(scores - top), axis=-1, keepdims=True)))
        shares = rounded(jnp.exp(scores - log_total))
        mixed = jnp.einsum('hqk,khd->qhd', shares, value_heads)
        return (mixed.reshape(span, D).astype(jnp.bfloat16), log_total[:, :, 0].T)
    mixed, log_totals = lax.map(one_block, jnp.arange(LENGTH // span, dtype=jnp.int32))
    return (mixed.reshape(LENGTH, D), log_totals.reshape(LENGTH, HEADS))

def attend_back(query, keys, values, mixed, log_totals, mixed_grad, places, start_prefix):
    scale = HEAD_DIM ** (-0.5)
    span = min(512, LENGTH)
    query_heads = query.astype(jnp.float32).reshape(LENGTH, HEADS, HEAD_DIM)
    key_heads = keys.astype(jnp.float32).reshape(LENGTH, HEADS, HEAD_DIM)
    value_heads = values.astype(jnp.float32).reshape(LENGTH, HEADS, HEAD_DIM)
    upper_heads = mixed_grad.astype(jnp.float32).reshape(LENGTH, HEADS, HEAD_DIM)
    flows = lax.optimization_barrier(jnp.sum(upper_heads * mixed.astype(jnp.float32).reshape(LENGTH, HEADS, HEAD_DIM), axis=-1))
    limits = jnp.maximum(places, start_prefix - 1)

    def one_block(state, number):
        key_grad, value_grad = state
        start = number * span
        part = lax.dynamic_slice_in_dim(query_heads, start, span, 0)
        above = lax.dynamic_slice_in_dim(upper_heads, start, span, 0)
        limit = lax.dynamic_slice_in_dim(limits, start, span, 0)
        log_part = lax.dynamic_slice_in_dim(log_totals, start, span, 0)
        flow_part = lax.dynamic_slice_in_dim(flows, start, span, 0)
        scores = jnp.einsum('qhd,khd->hqk', part, key_heads) * scale
        visible = places[None, None, :] <= limit[None, :, None]
        scores = jnp.where(visible, scores, NEGATIVE)
        shares = jnp.exp(scores - log_part.T[:, :, None])
        share_grad = jnp.einsum('qhd,khd->hqk', above, value_heads)
        score_grad = shares * (share_grad - flow_part.T[:, :, None])
        score_round = rounded(score_grad)
        share_round = rounded(shares)
        query_grad = jnp.einsum('hqk,khd->qhd', score_round, key_heads) * scale
        key_grad = key_grad + jnp.einsum('hqk,qhd->khd', score_round, part) * scale
        value_grad = value_grad + jnp.einsum('hqk,qhd->khd', share_round, above)
        return ((key_grad, value_grad), query_grad.reshape(span, D))
    zero_heads = jnp.zeros((LENGTH, HEADS, HEAD_DIM), jnp.float32)
    (key_grad, value_grad), query_grads = lax.scan(one_block, (zero_heads, zero_heads), jnp.arange(LENGTH // span, dtype=jnp.int32))
    return (query_grads.reshape(LENGTH, D), key_grad.reshape(LENGTH, D), value_grad.reshape(LENGTH, D))

def reference(block_input, positions, prefix, first_gain, first_bias, query_key_value, query_value_bias, output_weight, output_bias, second_gain, second_bias, expand_weight, expand_bias, contract_weight, contract_bias, cotangent):

    def one_sequence(state, items):
        rows_in, places, start_prefix, upper = items
        input_rows = rows_in.astype(jnp.float32)
        first_out, first_normed, first_inverse = layer_norm(input_rows, first_gain, first_bias)
        first_round = first_out.astype(jnp.bfloat16)
        joint = jnp.dot(first_round, query_key_value, preferred_element_type=jnp.float32)
        query = (joint[:, :D] + query_value_bias[0]).astype(jnp.bfloat16)
        keys = joint[:, D:2 * D].astype(jnp.bfloat16)
        values = (joint[:, 2 * D:] + query_value_bias[1]).astype(jnp.bfloat16)
        mixed, log_totals = attend(query, keys, values, places, start_prefix)
        residual = input_rows + jnp.dot(mixed, output_weight, preferred_element_type=jnp.float32) + output_bias
        second_out, second_normed, second_inverse = layer_norm(residual, second_gain, second_bias)
        second_round = second_out.astype(jnp.bfloat16)
        before = jnp.dot(second_round, expand_weight, preferred_element_type=jnp.float32) + expand_bias
        after, gelu_back = jax.vjp(gelu, before)
        after_round = after.astype(jnp.bfloat16)
        output = (residual + jnp.dot(after_round, contract_weight, preferred_element_type=jnp.float32) + contract_bias).astype(jnp.bfloat16)
        upper_wide = upper.astype(jnp.float32)
        after_grad = jnp.dot(upper, contract_weight.T, preferred_element_type=jnp.float32)
        before_grad = gelu_back(after_grad)[0]
        before_round = before_grad.astype(jnp.bfloat16)
        second_grad = jnp.dot(before_round, expand_weight.T, preferred_element_type=jnp.float32)
        residual_grad = upper_wide + norm_back(second_grad, second_normed, second_inverse, second_gain)
        residual_round = residual_grad.astype(jnp.bfloat16)
        mixed_grad = jnp.dot(residual_round, output_weight.T, preferred_element_type=jnp.float32).astype(jnp.bfloat16)
        query_grad, key_grad, value_grad = attend_back(query, keys, values, mixed, log_totals, mixed_grad, places, start_prefix)
        joint_grad = jnp.concatenate([query_grad, key_grad, value_grad], axis=1).astype(jnp.bfloat16)
        first_grad = jnp.dot(joint_grad, query_key_value.T, preferred_element_type=jnp.float32)
        input_gradient = residual_grad + norm_back(first_grad, first_normed, first_inverse, first_gain)
        terms = (lax.optimization_barrier(jnp.sum(first_grad * first_normed, axis=0)), lax.optimization_barrier(jnp.sum(first_grad, axis=0)), jnp.dot(first_round.T, joint_grad, preferred_element_type=jnp.float32), jnp.stack([lax.optimization_barrier(jnp.sum(query_grad, axis=0)), lax.optimization_barrier(jnp.sum(value_grad, axis=0))]), jnp.dot(mixed.T, residual_round, preferred_element_type=jnp.float32), lax.optimization_barrier(jnp.sum(residual_grad, axis=0)), lax.optimization_barrier(jnp.sum(second_grad * second_normed, axis=0)), lax.optimization_barrier(jnp.sum(second_grad, axis=0)), jnp.dot(second_round.T, before_round, preferred_element_type=jnp.float32), lax.optimization_barrier(jnp.sum(before_grad, axis=0)), jnp.dot(after_round.T, upper, preferred_element_type=jnp.float32), lax.optimization_barrier(jnp.sum(upper_wide, axis=0)))
        new_state = tuple((earlier + added for earlier, added in zip(state, terms)))
        return (new_state, (output, input_gradient))
    start_state = (jnp.zeros((D,), jnp.float32), jnp.zeros((D,), jnp.float32), jnp.zeros((D, 3 * D), jnp.float32), jnp.zeros((2, D), jnp.float32), jnp.zeros((D, D), jnp.float32), jnp.zeros((D,), jnp.float32), jnp.zeros((D,), jnp.float32), jnp.zeros((D,), jnp.float32), jnp.zeros((D, FF), jnp.float32), jnp.zeros((FF,), jnp.float32), jnp.zeros((FF, D), jnp.float32), jnp.zeros((D,), jnp.float32))
    final, (outputs, input_grads) = lax.scan(one_sequence, start_state, (block_input, positions, prefix, cotangent))
    return (outputs, input_grads, final[0], final[1], final[2], final[3], final[4], final[5], final[6], final[7], final[8], final[9], final[10], final[11])
```

```python
import jax
import jax.numpy as jnp
from jax import lax
from jax.sharding import PartitionSpec as P

HEAD_DIM = 64
EPSILON = 1e-05
NEGATIVE = -1e30
LOW = 64


def layer_norm(values, gain, bias):
    center = values - jnp.mean(values, axis=-1, keepdims=True)
    inverse = lax.rsqrt(jnp.mean(center * center, axis=-1, keepdims=True) + EPSILON)
    normed = center * inverse
    return (normed * gain + bias, normed, inverse)


def norm_back(upper, normed, inverse, gain):
    scaled = upper * gain
    return inverse * (
        scaled
        - jnp.mean(scaled, axis=-1, keepdims=True)
        - normed * jnp.mean(scaled * normed, axis=-1, keepdims=True)
    )


def gelu(values):
    return jax.nn.gelu(values, approximate=True)


def term_of(left, right):
    return jnp.einsum("ti,tj->ij", left, right, preferred_element_type=jnp.float32)


def after(value, *earlier):
    return lax.optimization_barrier((value, *earlier))[0]


def swap(value, axis, size, step):
    return lax.ppermute(value, axis, [(i, i ^ step) for i in range(size)])


def gather_rows(shard, earlier):
    rows, columns = shard.shape
    half = rows // 2
    split = max(columns // 2 // 128, 1) * 128
    place = lax.axis_index("fsdp")
    core = lax.axis_index("ctx") % 2
    own = lax.dynamic_slice_in_dim(shard, core * half, half, 0)
    if earlier:
        own = after(own, *earlier)
    along_x = swap(own, "fsdp", 4, 1)
    along_y = swap(own, "fsdp", 4, 2)
    far_x = swap(along_x[:, :split], "fsdp", 4, 2)
    far_y = swap(along_y[:, split:], "fsdp", 4, 1)
    full = jnp.zeros((4 * rows, columns), shard.dtype)
    full = lax.dynamic_update_slice(full, shard, (place * rows, 0))
    mine = ((along_x, 1, 0), (along_y, 2, 0), (far_x, 3, 0), (far_y, 3, split))
    for piece, step, column in mine:
        full = lax.dynamic_update_slice(full, piece, ((place ^ step) * rows + core * half, column))
    for piece, step, column in mine:
        other = swap(piece, "ctx", 8, 1)
        start = (place ^ step) * rows + (1 - core) * half
        full = lax.dynamic_update_slice(full, other, (start, column))
    return full, (along_x, along_y)


def spread_tokens(local):
    columns = local.shape[1]
    split = max(columns // 2 // 128, 1) * 128
    along_x = swap(local, "fsdp", 4, 1)
    along_y = swap(local, "fsdp", 4, 2)
    far_x = swap(along_x[:, :split], "fsdp", 4, 2)
    far_y = swap(along_y[:, split:], "fsdp", 4, 1)
    return jnp.concatenate(
        [local, along_x, along_y, jnp.concatenate([far_x, far_y], axis=1)], axis=0
    )


def ctx_sum(part, columns, by_rows):
    rows, padded = part.shape
    half = rows // 2
    number = lax.axis_index("ctx")
    core = number % 2
    level = number // 2
    sent = lax.dynamic_slice_in_dim(part, (1 - core) * half, half, 0).astype(jnp.bfloat16)
    kept = lax.dynamic_slice_in_dim(part, core * half, half, 0)
    kept = kept + swap(sent, "ctx", 8, 1).astype(jnp.float32)
    axis = 0 if by_rows else 1
    width = kept.shape[axis] // 4

    def block(step):
        return lax.dynamic_slice_in_dim(kept, (level ^ step) * width, width, axis)

    total = block(0)
    for step in (1, 2, 3):
        total = total + swap(block(step).astype(jnp.bfloat16), "ctx", 8, 2 * step).astype(
            jnp.float32
        )
    total = lax.optimization_barrier(total.astype(jnp.bfloat16))
    whole = jnp.zeros((half, padded), jnp.bfloat16)
    whole = lax.dynamic_update_slice_in_dim(whole, total, level * width, axis)
    for step in (1, 2, 3):
        piece = swap(total, "ctx", 8, 2 * step)
        whole = lax.dynamic_update_slice_in_dim(whole, piece, (level ^ step) * width, axis)
    other = swap(whole, "ctx", 8, 1)
    first = jnp.where(core == 0, whole, other)
    second = jnp.where(core == 0, other, whole)
    return jnp.concatenate([first, second], axis=0)[:, :columns].astype(jnp.float32)


def all_sum(values, fast):
    if not fast:
        return lax.psum(values, ("fsdp", "ctx"))
    shape = values.shape
    values = values.reshape(-1, 128)
    for axis, size, step in (
        ("ctx", 8, 1),
        ("fsdp", 4, 1),
        ("fsdp", 4, 2),
        ("ctx", 8, 2),
        ("ctx", 8, 4),
    ):
        values = values + swap(values, axis, size, step)
    return values.reshape(shape)


def per_device(
    parts,
    spans,
    block_input,
    positions,
    prefix,
    first_gain,
    first_bias,
    query_key_value,
    query_value_bias,
    output_weight,
    output_bias,
    second_gain,
    second_bias,
    expand_weight,
    expand_bias,
    contract_weight,
    contract_bias,
    cotangent,
):
    fast = parts == 4 and spans == 8
    sequences, piece, width = block_input.shape
    hidden = expand_weight.shape[1]
    heads = width // HEAD_DIM
    scale = HEAD_DIM ** (-0.5)
    rows = sequences * piece
    length = spans * piece
    slots = -(-sequences * heads // spans)
    band = slots * HEAD_DIM
    number = lax.axis_index("ctx")

    if fast:
        joint_full, near = gather_rows(query_key_value, ())
        output_full, near = gather_rows(output_weight, near)
        expand_full, near = gather_rows(expand_weight, near)
        contract_full, near = gather_rows(contract_weight, near)
    else:
        joint_full, output_full, expand_full, contract_full = (
            lax.all_gather(w, "fsdp", axis=0, tiled=True)
            for w in (query_key_value, output_weight, expand_weight, contract_weight)
        )

    def to_bands(tensors):
        wide = []
        for tensor in tensors:
            flat = jnp.swapaxes(tensor.reshape(sequences, piece, width), 0, 1)
            flat = flat.reshape(piece, sequences * width)
            flat = jnp.pad(flat, ((0, 0), (0, spans * band - sequences * width)))
            wide.append(flat.reshape(piece, spans, band))
        joined = jnp.concatenate(wide, axis=2) if len(wide) > 1 else wide[0]
        return jnp.swapaxes(joined, 0, 1)

    def from_bands(blocks, count):
        flat = blocks.reshape(spans, piece, count, band).transpose(1, 2, 0, 3)
        flat = flat.reshape(piece, count, spans * band)[:, :, : sequences * width]
        flat = flat.reshape(piece, count, sequences, width).transpose(2, 0, 1, 3)
        return flat.reshape(rows, count * width)

    def exchange(blocks):
        return lax.all_to_all(blocks, "ctx", 0, 0, tiled=True)

    def heads_of(flat, count):
        return flat.reshape(length, count, slots, HEAD_DIM).transpose(1, 2, 0, 3)

    input_rows = block_input.reshape(rows, width).astype(jnp.float32)
    first_out, first_normed, first_inverse = layer_norm(input_rows, first_gain, first_bias)
    first_round = first_out.astype(jnp.bfloat16)
    joint = jnp.dot(first_round, joint_full, preferred_element_type=jnp.float32)
    query = (joint[:, :width] + query_value_bias[0]).astype(jnp.bfloat16)
    keys = joint[:, width : 2 * width].astype(jnp.bfloat16)
    values = (joint[:, 2 * width :] + query_value_bias[1]).astype(jnp.bfloat16)
    digits = jnp.concatenate([positions // LOW, positions % LOW], axis=0).T.astype(jnp.bfloat16)
    digits = jnp.broadcast_to(digits[None], (spans, piece, 2 * sequences))
    received = exchange(jnp.concatenate([to_bands((query, keys, values)), digits], axis=2))
    received = received.reshape(length, 3 * band + 2 * sequences)
    query_heads, key_heads, value_heads = heads_of(received[:, : 3 * band], 3)
    digits = received[:, 3 * band :].astype(jnp.int32)
    places = digits[:, :sequences].T * LOW + digits[:, sequences:].T
    limits = jnp.maximum(places, prefix[:, None] - 1)
    owner = jnp.minimum((number * slots + jnp.arange(slots)) // heads, sequences - 1)

    def of_owner(table):
        chosen = jnp.broadcast_to(table[0][None], (slots, length))
        for row in range(1, sequences):
            chosen = jnp.where(owner[:, None] == row, table[row][None], chosen)
        return chosen

    visible = of_owner(places)[:, None, :] <= of_owner(limits)[:, :, None]
    scores = (
        jnp.einsum("pqd,pkd->pqk", query_heads, key_heads, preferred_element_type=jnp.float32)
        * scale
    )
    scores = jnp.where(visible, scores, NEGATIVE)
    top = jnp.max(scores, axis=-1, keepdims=True)
    log_total = top + jnp.log(jnp.sum(jnp.exp(scores - top), axis=-1, keepdims=True))
    chance = jnp.exp(scores - log_total)
    shares = chance.astype(jnp.bfloat16)
    mixed_heads = jnp.einsum(
        "pqk,pkd->pqd", shares, value_heads, preferred_element_type=jnp.float32
    ).astype(jnp.bfloat16)

    def to_pieces(tensor):
        return tensor.transpose(1, 0, 2).reshape(spans, piece, band)

    mixed = from_bands(exchange(to_pieces(mixed_heads)), 1)
    residual = (
        input_rows + jnp.dot(mixed, output_full, preferred_element_type=jnp.float32) + output_bias
    )
    second_out, second_normed, second_inverse = layer_norm(residual, second_gain, second_bias)
    second_round = second_out.astype(jnp.bfloat16)
    before = jnp.dot(second_round, expand_full, preferred_element_type=jnp.float32) + expand_bias
    activated, gelu_back = jax.vjp(gelu, before)
    after_round = activated.astype(jnp.bfloat16)
    block_output = (
        (
            residual
            + jnp.dot(after_round, contract_full, preferred_element_type=jnp.float32)
            + contract_bias
        )
        .astype(jnp.bfloat16)
        .reshape(sequences, piece, width)
    )
    upper = cotangent.reshape(rows, width)
    upper_wide = upper.astype(jnp.float32)
    after_grad = jnp.dot(upper, contract_full.T, preferred_element_type=jnp.float32)
    before_grad = gelu_back(after_grad)[0]
    before_round = before_grad.astype(jnp.bfloat16)
    second_grad = jnp.dot(before_round, expand_full.T, preferred_element_type=jnp.float32)
    residual_grad = upper_wide + norm_back(second_grad, second_normed, second_inverse, second_gain)
    residual_round = residual_grad.astype(jnp.bfloat16)
    mixed_grad = jnp.dot(residual_round, output_full.T, preferred_element_type=jnp.float32).astype(
        jnp.bfloat16
    )

    above = heads_of(exchange(to_bands((mixed_grad,))).reshape(length, band), 1)[0]
    flows = jnp.sum(
        above.astype(jnp.float32) * mixed_heads.astype(jnp.float32), axis=-1, keepdims=True
    )
    share_grad = jnp.einsum("pqd,pkd->pqk", above, value_heads, preferred_element_type=jnp.float32)
    score_round = (chance * (share_grad - flows)).astype(jnp.bfloat16)
    query_grad = (
        jnp.einsum("pqk,pkd->pqd", score_round, key_heads, preferred_element_type=jnp.float32)
        * scale
    )
    key_grad = (
        jnp.einsum("pqk,pqd->pkd", score_round, query_heads, preferred_element_type=jnp.float32)
        * scale
    )
    value_grad = jnp.einsum("pqk,pqd->pkd", shares, above, preferred_element_type=jnp.float32)
    pieces = [to_pieces(g.astype(jnp.bfloat16)) for g in (query_grad, key_grad, value_grad)]
    joint_grad = from_bands(exchange(jnp.concatenate(pieces, axis=2)), 3)

    def bias_sum(grad):
        line = jnp.zeros((spans * band,), jnp.float32)
        line = lax.dynamic_update_slice(line, jnp.sum(grad, axis=1).reshape(band), (number * band,))
        return jnp.sum(line[: sequences * width].reshape(sequences, width), axis=0)

    first_grad = jnp.dot(joint_grad, joint_full.T, preferred_element_type=jnp.float32)
    input_gradient = (
        residual_grad + norm_back(first_grad, first_normed, first_inverse, first_gain)
    ).reshape(sequences, piece, width)

    if fast:
        place = lax.axis_index("fsdp")
        narrow = width // parts
        broad = hidden // parts
        lefts = jnp.concatenate(
            [
                x.reshape(rows, parts, x.shape[1] // parts)
                for x in (after_round, first_round, mixed, second_round)
            ],
            axis=2,
        )
        lefts = jnp.swapaxes(lefts, 0, 1)
        picked = [lax.dynamic_index_in_dim(lefts, place ^ s, 0, False) for s in range(4)]
        left = jnp.concatenate(
            [picked[0]] + [swap(picked[s], "fsdp", 4, s) for s in (1, 2, 3)], axis=0
        )
        after_left = left[:, :broad]
        first_left = left[:, broad : broad + narrow]
        mixed_left = left[:, broad + narrow : broad + 2 * narrow]
        second_left = left[:, broad + 2 * narrow :]

        def grad_of(rows_left, right):
            columns = right.shape[1]
            padded = -(-columns // 512) * 512
            right = jnp.pad(spread_tokens(right), ((0, 0), (0, padded - columns)))
            return ctx_sum(term_of(rows_left, right), columns, False)

        contract_sum = ctx_sum(term_of(after_left, spread_tokens(upper)), width, True)
        expand_sum = grad_of(second_left, before_round)
        output_sum = grad_of(mixed_left, residual_round)
        joint_sum = grad_of(first_left, joint_grad)
    else:
        joint_sum, output_sum, expand_sum, contract_sum = (
            lax.psum(
                lax.psum_scatter(term_of(x, y), "fsdp", scatter_dimension=0, tiled=True), "ctx"
            )
            for x, y in (
                (first_round, joint_grad),
                (mixed, residual_round),
                (second_round, before_round),
                (after_round, upper),
            )
        )
    early = all_sum(
        jnp.concatenate(
            [
                jnp.sum(residual_grad, axis=0),
                jnp.sum(second_grad * second_normed, axis=0),
                jnp.sum(second_grad, axis=0),
                jnp.sum(upper_wide, axis=0),
                jnp.sum(before_grad, axis=0),
            ]
        ),
        fast,
    )
    late = all_sum(
        jnp.concatenate(
            [
                jnp.sum(first_grad * first_normed, axis=0),
                jnp.sum(first_grad, axis=0),
                bias_sum(query_grad),
                bias_sum(value_grad),
            ]
        ),
        fast,
    )
    return (
        block_output,
        input_gradient,
        late[:width],
        late[width : 2 * width],
        joint_sum,
        late[2 * width :].reshape(2, width),
        output_sum,
        early[:width],
        early[width : 2 * width],
        early[2 * width : 3 * width],
        expand_sum,
        early[4 * width :],
        contract_sum,
        early[3 * width : 4 * width],
    )


def solution(mesh):
    parts, spans = mesh.shape["fsdp"], mesh.shape["ctx"]
    in_specs = (
        P("fsdp", "ctx", None),
        P("fsdp", "ctx"),
        P("fsdp"),
        P(),
        P(),
        P("fsdp", None),
        P(),
        P("fsdp", None),
        P(),
        P(),
        P(),
        P("fsdp", None),
        P(),
        P("fsdp", None),
        P(),
        P("fsdp", "ctx", None),
    )
    out_specs = (
        P("fsdp", "ctx", None),
        P("fsdp", "ctx", None),
        P(),
        P(),
        P("fsdp", None),
        P(),
        P("fsdp", None),
        P(),
        P(),
        P(),
        P("fsdp", None),
        P(),
        P("fsdp", None),
        P(),
    )

    def body(*args):
        return per_device(parts, spans, *args)

    return jax.shard_map(body, mesh=mesh, in_specs=in_specs, out_specs=out_specs, check_vma=False)
```

```python
import jax
import jax.numpy as jnp
from jax import lax
from jax.sharding import PartitionSpec as P

HEAD_DIM = 64
EPSILON = 1e-05
NEGATIVE = -1e30
LOW = 64


def layer_norm(values, gain, bias):
    center = values - jnp.mean(values, axis=-1, keepdims=True)
    inverse = lax.rsqrt(jnp.mean(center * center, axis=-1, keepdims=True) + EPSILON)
    normed = center * inverse
    return (normed * gain + bias, normed, inverse)


def norm_back(upper, normed, inverse, gain):
    scaled = upper * gain
    return inverse * (
        scaled
        - jnp.mean(scaled, axis=-1, keepdims=True)
        - normed * jnp.mean(scaled * normed, axis=-1, keepdims=True)
    )


def gelu(values):
    return jax.nn.gelu(values, approximate=True)


def term_of(left, right):
    return jnp.einsum("ti,tj->ij", left, right, preferred_element_type=jnp.float32)


def gate(values, *milestones):
    return lax.optimization_barrier((*values, *milestones))[: len(values)]


def swap(value, axis, size, step):
    return lax.ppermute(value, axis, [(i, i ^ step) for i in range(size)])


def middle(columns):
    return max(columns // 2 // 128, 1) * 128


def near_rows(local):
    return swap(local, "fsdp", 4, 1), swap(local, "fsdp", 4, 2)


def far_rows(along_x, along_y):
    split = middle(along_x.shape[1])
    return swap(along_x[:, :split], "fsdp", 4, 2), swap(along_y[:, split:], "fsdp", 4, 1)


def own_half(shard):
    half = shard.shape[0] // 2
    return lax.dynamic_slice_in_dim(shard, (lax.axis_index("ctx") % 2) * half, half, 0)


def assemble(shard, near, far):
    rows, columns = shard.shape
    half = rows // 2
    place = lax.axis_index("fsdp")
    core = lax.axis_index("ctx") % 2
    full = jnp.zeros((4 * rows, columns), shard.dtype)
    full = lax.dynamic_update_slice(full, shard, (place * rows, 0))
    mine = ((near[0], 1, 0), (near[1], 2, 0), (far[0], 3, 0), (far[1], 3, middle(columns)))
    others = [swap(piece, "ctx", 8, 1) for piece, _, _ in mine]
    for piece, step, column in mine:
        full = lax.dynamic_update_slice(full, piece, ((place ^ step) * rows + core * half, column))
    for other, (_, step, column) in zip(others, mine):
        start = (place ^ step) * rows + (1 - core) * half
        full = lax.dynamic_update_slice(full, other, (start, column))
    return full


def stacked(local, near, far):
    return jnp.concatenate([local, *near, jnp.concatenate(far, axis=1)], axis=0)


def placed(bit, mine, other, axis):
    first = jnp.where(bit == 0, mine, other)
    second = jnp.where(bit == 0, other, mine)
    return jnp.concatenate([first, second], axis=axis)


def level_bits():
    number = lax.axis_index("ctx")
    return number % 2, (number // 2) % 2, number // 4


def core_sum(part):
    core = level_bits()[0]
    half = part.shape[0] // 2
    sent = lax.dynamic_slice_in_dim(part, (1 - core) * half, half, 0).astype(jnp.bfloat16)
    kept = lax.dynamic_slice_in_dim(part, core * half, half, 0)
    return kept + swap(sent, "ctx", 8, 1).astype(jnp.float32)


def fold(kept, bit, step, axis):
    width = kept.shape[axis] // 2
    sent = lax.dynamic_slice_in_dim(kept, (1 - bit) * width, width, axis).astype(jnp.bfloat16)
    mine = lax.dynamic_slice_in_dim(kept, bit * width, width, axis)
    return mine + swap(sent, "ctx", 8, step).astype(jnp.float32)


def ctx_sum(part, columns, axis, gates):
    core, low, high = level_bits()
    total = core_sum(part)
    (total,) = gate((total,), *gates[0])
    total = fold(total, low, 2, axis)
    (total,) = gate((total,), *gates[1])
    total = fold(total, high, 4, axis)
    (total,) = gate((total.astype(jnp.bfloat16),), *gates[2])
    total = placed(high, total, swap(total, "ctx", 8, 4), axis)
    (total,) = gate((total,), *gates[3])
    total = placed(low, total, swap(total, "ctx", 8, 2), axis)
    (total,) = gate((total,), *gates[4])
    total = placed(core, total, swap(total, "ctx", 8, 1), 0)
    return total[:, :columns].astype(jnp.float32)


def all_sum(values, fast):
    if not fast:
        return lax.psum(values, ("fsdp", "ctx"))
    shape = values.shape
    values = values.reshape(-1, 128)
    for axis, size, step in (
        ("ctx", 8, 1),
        ("fsdp", 4, 1),
        ("fsdp", 4, 2),
        ("ctx", 8, 2),
        ("ctx", 8, 4),
    ):
        values = values + swap(values, axis, size, step)
    return values.reshape(shape)


def per_device(
    parts,
    spans,
    block_input,
    positions,
    prefix,
    first_gain,
    first_bias,
    query_key_value,
    query_value_bias,
    output_weight,
    output_bias,
    second_gain,
    second_bias,
    expand_weight,
    expand_bias,
    contract_weight,
    contract_bias,
    cotangent,
):
    fast = parts == 4 and spans == 8
    sequences, piece, width = block_input.shape
    hidden = expand_weight.shape[1]
    heads = width // HEAD_DIM
    scale = HEAD_DIM ** (-0.5)
    rows = sequences * piece
    length = spans * piece
    slots = -(-sequences * heads // spans)
    band = slots * HEAD_DIM
    number = lax.axis_index("ctx")

    if fast:
        joint_near = near_rows(own_half(query_key_value))
        joint_far = far_rows(*joint_near)
        joint_full = assemble(query_key_value, joint_near, joint_far)
        output_half, expand_half, contract_half = gate(
            (own_half(output_weight), own_half(expand_weight), own_half(contract_weight)),
            *joint_far,
        )
        output_near = near_rows(output_half)
        expand_near = near_rows(expand_half)
    else:
        joint_full, output_full, expand_full, contract_full = (
            lax.all_gather(w, "fsdp", axis=0, tiled=True)
            for w in (query_key_value, output_weight, expand_weight, contract_weight)
        )

    def to_bands(tensors):
        wide = []
        for tensor in tensors:
            flat = [tensor[s * piece : (s + 1) * piece] for s in range(sequences)]
            flat.append(jnp.zeros((piece, spans * band - sequences * width), tensor.dtype))
            wide.append(jnp.concatenate(flat, axis=1))
        blocks = [
            jnp.concatenate([w[:, j * band : (j + 1) * band] for w in wide], axis=1)
            for j in range(spans)
        ]
        return jnp.stack(blocks)

    def from_bands(blocks, count):
        whole = []
        for t in range(count):
            flat = jnp.concatenate(
                [blocks[j, :, t * band : (t + 1) * band] for j in range(spans)], axis=1
            )
            whole.append(
                jnp.concatenate(
                    [flat[:, s * width : (s + 1) * width] for s in range(sequences)], axis=0
                )
            )
        return jnp.concatenate(whole, axis=1)

    def exchange(blocks):
        return lax.all_to_all(blocks, "ctx", 0, 0, tiled=True)

    def heads_of(flat, number_of):
        starts = [number_of * band + i * HEAD_DIM for i in range(slots)]
        return jnp.stack([flat[:, start : start + HEAD_DIM] for start in starts])

    input_rows = block_input.reshape(rows, width).astype(jnp.float32)
    first_out, first_normed, first_inverse = layer_norm(input_rows, first_gain, first_bias)
    first_round = first_out.astype(jnp.bfloat16)
    joint = jnp.dot(first_round, joint_full, preferred_element_type=jnp.float32)
    query = (joint[:, :width] + query_value_bias[0]).astype(jnp.bfloat16)
    keys = joint[:, width : 2 * width].astype(jnp.bfloat16)
    values = (joint[:, 2 * width :] + query_value_bias[1]).astype(jnp.bfloat16)
    digits = jnp.concatenate([positions // LOW, positions % LOW], axis=0).T.astype(jnp.bfloat16)
    digits = jnp.broadcast_to(digits[None], (spans, piece, 2 * sequences))
    payload = jnp.concatenate([to_bands((query, keys, values)), digits], axis=2)
    if fast:
        output_near = gate(output_near, payload)
        expand_near = gate(expand_near, payload)
        output_far = far_rows(*output_near)
        expand_far = far_rows(*expand_near)
        contract_near = near_rows(gate((contract_half,), *expand_near)[0])
    received = exchange(payload)
    received = received.reshape(length, 3 * band + 2 * sequences)
    query_heads, key_heads, value_heads = (heads_of(received, t) for t in range(3))
    digits = received[:, 3 * band :].astype(jnp.int32)
    places = digits[:, :sequences].T * LOW + digits[:, sequences:].T
    limits = jnp.maximum(places, prefix[:, None] - 1)
    owner = jnp.minimum((number * slots + jnp.arange(slots)) // heads, sequences - 1)

    def of_owner(table):
        chosen = jnp.broadcast_to(table[0][None], (slots, length))
        for row in range(1, sequences):
            chosen = jnp.where(owner[:, None] == row, table[row][None], chosen)
        return chosen

    visible = of_owner(places)[:, None, :] <= of_owner(limits)[:, :, None]
    scores = (
        jnp.einsum("pqd,pkd->pqk", query_heads, key_heads, preferred_element_type=jnp.float32)
        * scale
    )
    scores = jnp.where(visible, scores, NEGATIVE)
    top = jnp.max(scores, axis=-1, keepdims=True)
    log_total = top + jnp.log(jnp.sum(jnp.exp(scores - top), axis=-1, keepdims=True))
    chance = jnp.exp(scores - log_total)
    shares = chance.astype(jnp.bfloat16)
    mixed_heads = jnp.einsum(
        "pqk,pkd->pqd", shares, value_heads, preferred_element_type=jnp.float32
    ).astype(jnp.bfloat16)

    def to_pieces(tensor):
        return jnp.concatenate([tensor[i] for i in range(slots)], axis=1).reshape(
            spans, piece, band
        )

    mixed_pieces = to_pieces(mixed_heads)
    upper = cotangent.reshape(rows, width)
    if fast:
        output_far = gate(output_far, mixed_pieces)
        expand_far = gate(expand_far, mixed_pieces)
        contract_near = gate(contract_near, mixed_pieces)
        output_full = assemble(output_weight, output_near, output_far)
        expand_full = assemble(expand_weight, expand_near, expand_far)
        contract_far = far_rows(*contract_near)
        upper_near = near_rows(gate((upper,), *contract_near)[0])
    mixed = from_bands(exchange(mixed_pieces), 1)
    residual = (
        input_rows + jnp.dot(mixed, output_full, preferred_element_type=jnp.float32) + output_bias
    )
    second_out, second_normed, second_inverse = layer_norm(residual, second_gain, second_bias)
    second_round = second_out.astype(jnp.bfloat16)
    if fast:
        contract_far = gate(contract_far, second_round)
        contract_full = assemble(contract_weight, contract_near, contract_far)
        upper_near = gate(upper_near, second_round)
        upper_far = far_rows(*upper_near)
    before = jnp.dot(second_round, expand_full, preferred_element_type=jnp.float32) + expand_bias
    activated, gelu_back = jax.vjp(gelu, before)
    after_round = activated.astype(jnp.bfloat16)
    block_output = (
        (
            residual
            + jnp.dot(after_round, contract_full, preferred_element_type=jnp.float32)
            + contract_bias
        )
        .astype(jnp.bfloat16)
        .reshape(sequences, piece, width)
    )
    upper_wide = upper.astype(jnp.float32)
    after_grad = jnp.dot(upper, contract_full.T, preferred_element_type=jnp.float32)
    before_grad = gelu_back(after_grad)[0]
    before_round = before_grad.astype(jnp.bfloat16)
    second_grad = jnp.dot(before_round, expand_full.T, preferred_element_type=jnp.float32)
    residual_grad = upper_wide + norm_back(second_grad, second_normed, second_inverse, second_gain)
    residual_round = residual_grad.astype(jnp.bfloat16)
    mixed_grad = jnp.dot(residual_round, output_full.T, preferred_element_type=jnp.float32).astype(
        jnp.bfloat16
    )

    mixed_payload = to_bands((mixed_grad,))
    if fast:
        place = lax.axis_index("fsdp")
        narrow = width // parts
        broad = hidden // parts
        lefts = jnp.stack(
            [
                jnp.concatenate(
                    [
                        after_round[:, p * broad : (p + 1) * broad],
                        first_round[:, p * narrow : (p + 1) * narrow],
                        mixed[:, p * narrow : (p + 1) * narrow],
                        second_round[:, p * narrow : (p + 1) * narrow],
                    ],
                    axis=1,
                )
                for p in range(parts)
            ]
        )
        picked = [lax.dynamic_index_in_dim(lefts, place ^ s, 0, False) for s in range(4)]
        moved = [swap(picked[s], "fsdp", 4, s) for s in (1, 2, 3)]
        before_near = near_rows(before_round)
        residual_near = near_rows(residual_round)
        before_near = gate(before_near, mixed_payload)
        residual_near = gate(residual_near, mixed_payload)
        moved = gate(moved, mixed_payload)
        before_far = far_rows(*before_near)
        residual_far = far_rows(*residual_near)
        left = jnp.concatenate([picked[0], *moved], axis=0)
        after_left = left[:, :broad]
        first_left = left[:, broad : broad + narrow]
        mixed_left = left[:, broad + narrow : broad + 2 * narrow]
        second_left = left[:, broad + 2 * narrow :]
    above = heads_of(exchange(mixed_payload).reshape(length, band), 0)
    flows = jnp.sum(
        above.astype(jnp.float32) * mixed_heads.astype(jnp.float32), axis=-1, keepdims=True
    )
    share_grad = jnp.einsum("pqd,pkd->pqk", above, value_heads, preferred_element_type=jnp.float32)
    score_round = (chance * (share_grad - flows)).astype(jnp.bfloat16)
    query_grad = (
        jnp.einsum("pqk,pkd->pqd", score_round, key_heads, preferred_element_type=jnp.float32)
        * scale
    )
    key_grad = (
        jnp.einsum("pqk,pqd->pkd", score_round, query_heads, preferred_element_type=jnp.float32)
        * scale
    )
    value_grad = jnp.einsum("pqk,pqd->pkd", shares, above, preferred_element_type=jnp.float32)
    pieces = [to_pieces(g.astype(jnp.bfloat16)) for g in (query_grad, key_grad, value_grad)]
    joint_payload = jnp.concatenate(pieces, axis=2)
    joint_grad = from_bands(exchange(joint_payload), 3)

    def bias_sum(grad):
        line = jnp.zeros((spans * band,), jnp.float32)
        line = lax.dynamic_update_slice(line, jnp.sum(grad, axis=1).reshape(band), (number * band,))
        return jnp.sum(line[: sequences * width].reshape(sequences, width), axis=0)

    first_grad = jnp.dot(joint_grad, joint_full.T, preferred_element_type=jnp.float32)
    input_gradient = (
        residual_grad + norm_back(first_grad, first_normed, first_inverse, first_gain)
    ).reshape(sequences, piece, width)

    if fast:
        joint_near = near_rows(joint_grad)
        joint_far = far_rows(*joint_near)

        def grad_of(rows_left, right, gates):
            columns = right.shape[1]
            padded = -(-columns // 512) * 512
            right = jnp.pad(right, ((0, 0), (0, padded - columns)))
            return ctx_sum(term_of(rows_left, right), columns, 1, gates)

        contract_sum = ctx_sum(
            term_of(after_left, stacked(upper, upper_near, upper_far)),
            width,
            0,
            ((above,), (score_round,), (joint_payload,), (joint_grad,), joint_near),
        )
        before_far = gate(before_far, joint_payload)
        residual_far = gate(residual_far, joint_payload)
        side = ((), (joint_grad,), joint_near, joint_far, ())
        expand_sum = grad_of(second_left, stacked(before_round, before_near, before_far), side)
        output_sum = grad_of(mixed_left, stacked(residual_round, residual_near, residual_far), side)
        joint_sum = grad_of(first_left, stacked(joint_grad, joint_near, joint_far), ((),) * 5)
    else:
        joint_sum, output_sum, expand_sum, contract_sum = (
            lax.psum(
                lax.psum_scatter(term_of(x, y), "fsdp", scatter_dimension=0, tiled=True), "ctx"
            )
            for x, y in (
                (first_round, joint_grad),
                (mixed, residual_round),
                (second_round, before_round),
                (after_round, upper),
            )
        )
    small = all_sum(
        jnp.concatenate(
            [
                jnp.sum(residual_grad, axis=0),
                jnp.sum(second_grad * second_normed, axis=0),
                jnp.sum(second_grad, axis=0),
                jnp.sum(upper_wide, axis=0),
                jnp.sum(before_grad, axis=0),
                jnp.sum(first_grad * first_normed, axis=0),
                jnp.sum(first_grad, axis=0),
                bias_sum(query_grad),
                bias_sum(value_grad),
            ]
        ),
        fast,
    )
    early, late = small[: 4 * width + hidden], small[4 * width + hidden :]
    return (
        block_output,
        input_gradient,
        late[:width],
        late[width : 2 * width],
        joint_sum,
        late[2 * width :].reshape(2, width),
        output_sum,
        early[:width],
        early[width : 2 * width],
        early[2 * width : 3 * width],
        expand_sum,
        early[4 * width :],
        contract_sum,
        early[3 * width : 4 * width],
    )


def solution(mesh):
    parts, spans = mesh.shape["fsdp"], mesh.shape["ctx"]
    in_specs = (
        P("fsdp", "ctx", None),
        P("fsdp", "ctx"),
        P("fsdp"),
        P(),
        P(),
        P("fsdp", None),
        P(),
        P("fsdp", None),
        P(),
        P(),
        P(),
        P("fsdp", None),
        P(),
        P("fsdp", None),
        P(),
        P("fsdp", "ctx", None),
    )
    out_specs = (
        P("fsdp", "ctx", None),
        P("fsdp", "ctx", None),
        P(),
        P(),
        P("fsdp", None),
        P(),
        P("fsdp", None),
        P(),
        P(),
        P(),
        P("fsdp", None),
        P(),
        P("fsdp", None),
        P(),
    )

    def body(*args):
        return per_device(parts, spans, *args)

    return jax.shard_map(body, mesh=mesh, in_specs=in_specs, out_specs=out_specs, check_vma=False)
```

```python
import jax
import jax.numpy as jnp
from jax import lax
from jax.sharding import PartitionSpec as P

HEAD_DIM = 64
EPSILON = 1e-05
NEGATIVE = -1e30
LOW = 64


def layer_norm(values, gain, bias):
    center = values - jnp.mean(values, axis=-1, keepdims=True)
    inverse = lax.rsqrt(jnp.mean(center * center, axis=-1, keepdims=True) + EPSILON)
    normed = center * inverse
    return (normed * gain + bias, normed, inverse)


def norm_back(upper, normed, inverse, gain):
    scaled = upper * gain
    return inverse * (
        scaled
        - jnp.mean(scaled, axis=-1, keepdims=True)
        - normed * jnp.mean(scaled * normed, axis=-1, keepdims=True)
    )


def gelu(values):
    return jax.nn.gelu(values, approximate=True)


def term_of(left, right):
    return jnp.einsum("ti,tj->ij", left, right, preferred_element_type=jnp.float32)


def gate(values, *milestones):
    return lax.optimization_barrier((*values, *milestones))[: len(values)]


def swap(value, axis, size, step):
    return lax.ppermute(value, axis, [(i, i ^ step) for i in range(size)])


def middle(columns):
    return max(columns // 2 // 128, 1) * 128


def near_rows(local):
    return swap(local, "fsdp", 4, 1), swap(local, "fsdp", 4, 2)


def far_rows(along_x, along_y):
    split = middle(along_x.shape[1])
    return swap(along_x[:, :split], "fsdp", 4, 2), swap(along_y[:, split:], "fsdp", 4, 1)


def own_half(shard):
    half = shard.shape[0] // 2
    return lax.dynamic_slice_in_dim(shard, (lax.axis_index("ctx") % 2) * half, half, 0)


def assemble(shard, near, far):
    rows, columns = shard.shape
    half = rows // 2
    place = lax.axis_index("fsdp")
    core = lax.axis_index("ctx") % 2
    full = jnp.zeros((4 * rows, columns), shard.dtype)
    full = lax.dynamic_update_slice(full, shard, (place * rows, 0))
    mine = ((near[0], 1, 0), (near[1], 2, 0), (far[0], 3, 0), (far[1], 3, middle(columns)))
    others = [swap(piece, "ctx", 8, 1) for piece, _, _ in mine]
    for piece, step, column in mine:
        full = lax.dynamic_update_slice(full, piece, ((place ^ step) * rows + core * half, column))
    for other, (_, step, column) in zip(others, mine):
        start = (place ^ step) * rows + (1 - core) * half
        full = lax.dynamic_update_slice(full, other, (start, column))
    return full


def stacked(local, near, far):
    return jnp.concatenate([local, *near, jnp.concatenate(far, axis=1)], axis=0)


def placed(bit, mine, other, axis):
    first = jnp.where(bit == 0, mine, other)
    second = jnp.where(bit == 0, other, mine)
    return jnp.concatenate([first, second], axis=axis)


def level_bits():
    number = lax.axis_index("ctx")
    return number % 2, (number // 2) % 2, number // 4


def core_sum(part):
    core = level_bits()[0]
    half = part.shape[0] // 2
    sent = lax.dynamic_slice_in_dim(part, (1 - core) * half, half, 0).astype(jnp.bfloat16)
    kept = lax.dynamic_slice_in_dim(part, core * half, half, 0)
    return kept + swap(sent, "ctx", 8, 1).astype(jnp.float32)


def fold(kept, bit, step, axis):
    width = kept.shape[axis] // 2
    sent = lax.dynamic_slice_in_dim(kept, (1 - bit) * width, width, axis).astype(jnp.bfloat16)
    mine = lax.dynamic_slice_in_dim(kept, bit * width, width, axis)
    return mine + swap(sent, "ctx", 8, step).astype(jnp.float32)


def ctx_sum(part, columns, axis, gates):
    core, low, high = level_bits()
    total = core_sum(part)
    (total,) = gate((total,), *gates[0])
    total = fold(total, low, 2, axis)
    (total,) = gate((total,), *gates[1])
    total = fold(total, high, 4, axis)
    (total,) = gate((total.astype(jnp.bfloat16),), *gates[2])
    total = placed(high, total, swap(total, "ctx", 8, 4), axis)
    (total,) = gate((total,), *gates[3])
    total = placed(low, total, swap(total, "ctx", 8, 2), axis)
    (total,) = gate((total,), *gates[4])
    total = placed(core, total, swap(total, "ctx", 8, 1), 0)
    return total[:, :columns].astype(jnp.float32)


def all_sum(values, fast):
    if not fast:
        return lax.psum(values, ("fsdp", "ctx"))
    shape = values.shape
    values = values.reshape(-1, 128)
    values = values + swap(values, "ctx", 8, 1)
    for axis, size, unit in (("fsdp", 4, 1), ("ctx", 8, 2)):
        one, two, three = (swap(values, axis, size, step * unit) for step in (1, 2, 3))
        values = (values + one) + (two + three)
    return values.reshape(shape)


def per_device(
    parts,
    spans,
    block_input,
    positions,
    prefix,
    first_gain,
    first_bias,
    query_key_value,
    query_value_bias,
    output_weight,
    output_bias,
    second_gain,
    second_bias,
    expand_weight,
    expand_bias,
    contract_weight,
    contract_bias,
    cotangent,
):
    fast = parts == 4 and spans == 8
    sequences, piece, width = block_input.shape
    hidden = expand_weight.shape[1]
    heads = width // HEAD_DIM
    scale = HEAD_DIM ** (-0.5)
    rows = sequences * piece
    length = spans * piece
    slots = -(-sequences * heads // spans)
    band = slots * HEAD_DIM
    number = lax.axis_index("ctx")

    if fast:
        joint_near = near_rows(own_half(query_key_value))
        joint_far = far_rows(*joint_near)
        joint_full = assemble(query_key_value, joint_near, joint_far)
        output_half, expand_half, contract_half = gate(
            (own_half(output_weight), own_half(expand_weight), own_half(contract_weight)),
            *joint_far,
        )
        output_near = near_rows(output_half)
        expand_near = near_rows(expand_half)
    else:
        joint_full, output_full, expand_full, contract_full = (
            lax.all_gather(w, "fsdp", axis=0, tiled=True)
            for w in (query_key_value, output_weight, expand_weight, contract_weight)
        )

    def to_bands(tensors):
        wide = []
        for tensor in tensors:
            flat = [tensor[s * piece : (s + 1) * piece] for s in range(sequences)]
            flat.append(jnp.zeros((piece, spans * band - sequences * width), tensor.dtype))
            wide.append(jnp.concatenate(flat, axis=1))
        blocks = [
            jnp.concatenate([w[:, j * band : (j + 1) * band] for w in wide], axis=1)
            for j in range(spans)
        ]
        return jnp.stack(blocks)

    def from_bands(blocks, count):
        whole = []
        for t in range(count):
            flat = jnp.concatenate(
                [blocks[j, :, t * band : (t + 1) * band] for j in range(spans)], axis=1
            )
            whole.append(
                jnp.concatenate(
                    [flat[:, s * width : (s + 1) * width] for s in range(sequences)], axis=0
                )
            )
        return jnp.concatenate(whole, axis=1)

    def exchange(blocks):
        return lax.all_to_all(blocks, "ctx", 0, 0, tiled=True)

    def heads_of(flat, number_of):
        starts = [number_of * band + i * HEAD_DIM for i in range(slots)]
        return jnp.stack([flat[:, start : start + HEAD_DIM] for start in starts])

    input_rows = block_input.reshape(rows, width).astype(jnp.float32)
    first_out, first_normed, first_inverse = layer_norm(input_rows, first_gain, first_bias)
    first_round = first_out.astype(jnp.bfloat16)
    joint = jnp.dot(first_round, joint_full, preferred_element_type=jnp.float32)
    query = (joint[:, :width] + query_value_bias[0]).astype(jnp.bfloat16)
    keys = joint[:, width : 2 * width].astype(jnp.bfloat16)
    values = (joint[:, 2 * width :] + query_value_bias[1]).astype(jnp.bfloat16)
    digits = jnp.concatenate([positions // LOW, positions % LOW], axis=0).T.astype(jnp.bfloat16)
    digits = jnp.broadcast_to(digits[None], (spans, piece, 2 * sequences))
    payload = jnp.concatenate([to_bands((query, keys, values)), digits], axis=2)
    if fast:
        output_near = gate(output_near, payload)
        expand_near = gate(expand_near, payload)
        output_far = far_rows(*output_near)
        expand_far = far_rows(*expand_near)
        contract_near = near_rows(gate((contract_half,), *expand_near)[0])
    received = exchange(payload)
    received = received.reshape(length, 3 * band + 2 * sequences)
    query_heads, key_heads, value_heads = (heads_of(received, t) for t in range(3))
    digits = received[:, 3 * band :].astype(jnp.int32)
    places = digits[:, :sequences].T * LOW + digits[:, sequences:].T
    limits = jnp.maximum(places, prefix[:, None] - 1)
    owner = jnp.minimum((number * slots + jnp.arange(slots)) // heads, sequences - 1)

    def of_owner(table):
        chosen = jnp.broadcast_to(table[0][None], (slots, length))
        for row in range(1, sequences):
            chosen = jnp.where(owner[:, None] == row, table[row][None], chosen)
        return chosen

    visible = of_owner(places)[:, None, :] <= of_owner(limits)[:, :, None]
    scores = (
        jnp.einsum("pqd,pkd->pqk", query_heads, key_heads, preferred_element_type=jnp.float32)
        * scale
    )
    scores = jnp.where(visible, scores, NEGATIVE)
    top = jnp.max(scores, axis=-1, keepdims=True)
    log_total = top + jnp.log(jnp.sum(jnp.exp(scores - top), axis=-1, keepdims=True))
    chance = jnp.exp(scores - log_total)
    shares = chance.astype(jnp.bfloat16)
    mixed_heads = jnp.einsum(
        "pqk,pkd->pqd", shares, value_heads, preferred_element_type=jnp.float32
    ).astype(jnp.bfloat16)

    def to_pieces(tensor):
        return jnp.concatenate([tensor[i] for i in range(slots)], axis=1).reshape(
            spans, piece, band
        )

    mixed_pieces = to_pieces(mixed_heads)
    upper = cotangent.reshape(rows, width)
    if fast:
        output_far = gate(output_far, mixed_pieces)
        expand_far = gate(expand_far, mixed_pieces)
        contract_near = gate(contract_near, mixed_pieces)
        output_full = assemble(output_weight, output_near, output_far)
        expand_full = assemble(expand_weight, expand_near, expand_far)
        contract_far = far_rows(*contract_near)
        upper_near = near_rows(gate((upper,), *contract_near)[0])
    mixed = from_bands(exchange(mixed_pieces), 1)
    residual = (
        input_rows + jnp.dot(mixed, output_full, preferred_element_type=jnp.float32) + output_bias
    )
    second_out, second_normed, second_inverse = layer_norm(residual, second_gain, second_bias)
    second_round = second_out.astype(jnp.bfloat16)
    if fast:
        contract_far = gate(contract_far, second_round)
        contract_full = assemble(contract_weight, contract_near, contract_far)
        upper_near = gate(upper_near, second_round)
        upper_far = far_rows(*upper_near)
    before = jnp.dot(second_round, expand_full, preferred_element_type=jnp.float32) + expand_bias
    activated, gelu_back = jax.vjp(gelu, before)
    after_round = activated.astype(jnp.bfloat16)
    block_output = (
        (
            residual
            + jnp.dot(after_round, contract_full, preferred_element_type=jnp.float32)
            + contract_bias
        )
        .astype(jnp.bfloat16)
        .reshape(sequences, piece, width)
    )
    upper_wide = upper.astype(jnp.float32)
    after_grad = jnp.dot(upper, contract_full.T, preferred_element_type=jnp.float32)
    before_grad = gelu_back(after_grad)[0]
    before_round = before_grad.astype(jnp.bfloat16)
    second_grad = jnp.dot(before_round, expand_full.T, preferred_element_type=jnp.float32)
    residual_grad = upper_wide + norm_back(second_grad, second_normed, second_inverse, second_gain)
    residual_round = residual_grad.astype(jnp.bfloat16)
    mixed_grad = jnp.dot(residual_round, output_full.T, preferred_element_type=jnp.float32).astype(
        jnp.bfloat16
    )

    mixed_payload = to_bands((mixed_grad,))
    if fast:
        place = lax.axis_index("fsdp")
        narrow = width // parts
        broad = hidden // parts
        lefts = jnp.stack(
            [
                jnp.concatenate(
                    [
                        after_round[:, p * broad : (p + 1) * broad],
                        first_round[:, p * narrow : (p + 1) * narrow],
                        mixed[:, p * narrow : (p + 1) * narrow],
                        second_round[:, p * narrow : (p + 1) * narrow],
                    ],
                    axis=1,
                )
                for p in range(parts)
            ]
        )
        picked = [lax.dynamic_index_in_dim(lefts, place ^ s, 0, False) for s in range(4)]
        moved = [swap(picked[s], "fsdp", 4, s) for s in (1, 2, 3)]
        before_near = near_rows(before_round)
        residual_near = near_rows(residual_round)
        before_near = gate(before_near, mixed_payload)
        residual_near = gate(residual_near, mixed_payload)
        moved = gate(moved, mixed_payload)
        before_far = far_rows(*before_near)
        residual_far = far_rows(*residual_near)
        left = jnp.concatenate([picked[0], *moved], axis=0)
        after_left = left[:, :broad]
        first_left = left[:, broad : broad + narrow]
        mixed_left = left[:, broad + narrow : broad + 2 * narrow]
        second_left = left[:, broad + 2 * narrow :]
    above = heads_of(exchange(mixed_payload).reshape(length, band), 0)
    flows = jnp.sum(
        above.astype(jnp.float32) * mixed_heads.astype(jnp.float32), axis=-1, keepdims=True
    )
    share_grad = jnp.einsum("pqd,pkd->pqk", above, value_heads, preferred_element_type=jnp.float32)
    score_round = (chance * (share_grad - flows)).astype(jnp.bfloat16)
    query_grad = (
        jnp.einsum("pqk,pkd->pqd", score_round, key_heads, preferred_element_type=jnp.float32)
        * scale
    )
    key_grad = (
        jnp.einsum("pqk,pqd->pkd", score_round, query_heads, preferred_element_type=jnp.float32)
        * scale
    )
    value_grad = jnp.einsum("pqk,pqd->pkd", shares, above, preferred_element_type=jnp.float32)
    pieces = [to_pieces(g.astype(jnp.bfloat16)) for g in (query_grad, key_grad, value_grad)]
    joint_payload = jnp.concatenate(pieces, axis=2)
    joint_grad = from_bands(exchange(joint_payload), 3)

    def bias_sum(grad):
        line = jnp.zeros((spans * band,), jnp.float32)
        line = lax.dynamic_update_slice(line, jnp.sum(grad, axis=1).reshape(band), (number * band,))
        return jnp.sum(line[: sequences * width].reshape(sequences, width), axis=0)

    joint_later = joint_grad
    if fast:
        joint_near = near_rows(joint_grad)
        joint_far = far_rows(*joint_near)
        (joint_later,) = gate((joint_grad,), *joint_far)
    first_grad = jnp.dot(joint_later, joint_full.T, preferred_element_type=jnp.float32)
    input_gradient = (
        residual_grad + norm_back(first_grad, first_normed, first_inverse, first_gain)
    ).reshape(sequences, piece, width)

    if fast:

        def grad_of(rows_left, right, gates):
            columns = right.shape[1]
            padded = -(-columns // 512) * 512
            right = jnp.pad(right, ((0, 0), (0, padded - columns)))
            return ctx_sum(term_of(rows_left, right), columns, 1, gates)

        contract_sum = ctx_sum(
            term_of(after_left, stacked(upper, upper_near, upper_far)),
            width,
            0,
            ((above,), (score_round,), (joint_grad,), joint_near, joint_far),
        )
        before_far = gate(before_far, joint_payload)
        residual_far = gate(residual_far, joint_payload)
        side = ((joint_grad,), joint_near, joint_far, (), ())
        expand_sum = grad_of(second_left, stacked(before_round, before_near, before_far), side)
        output_sum = grad_of(mixed_left, stacked(residual_round, residual_near, residual_far), side)
        joint_sum = grad_of(first_left, stacked(joint_grad, joint_near, joint_far), ((),) * 5)
    else:
        joint_sum, output_sum, expand_sum, contract_sum = (
            lax.psum(
                lax.psum_scatter(term_of(x, y), "fsdp", scatter_dimension=0, tiled=True), "ctx"
            )
            for x, y in (
                (first_round, joint_grad),
                (mixed, residual_round),
                (second_round, before_round),
                (after_round, upper),
            )
        )
    small = all_sum(
        jnp.concatenate(
            [
                jnp.sum(residual_grad, axis=0),
                jnp.sum(second_grad * second_normed, axis=0),
                jnp.sum(second_grad, axis=0),
                jnp.sum(upper_wide, axis=0),
                jnp.sum(before_grad, axis=0),
                jnp.sum(first_grad * first_normed, axis=0),
                jnp.sum(first_grad, axis=0),
                bias_sum(query_grad),
                bias_sum(value_grad),
            ]
        ),
        fast,
    )
    early, late = small[: 4 * width + hidden], small[4 * width + hidden :]
    return (
        block_output,
        input_gradient,
        late[:width],
        late[width : 2 * width],
        joint_sum,
        late[2 * width :].reshape(2, width),
        output_sum,
        early[:width],
        early[width : 2 * width],
        early[2 * width : 3 * width],
        expand_sum,
        early[4 * width :],
        contract_sum,
        early[3 * width : 4 * width],
    )


def solution(mesh):
    parts, spans = mesh.shape["fsdp"], mesh.shape["ctx"]
    in_specs = (
        P("fsdp", "ctx", None),
        P("fsdp", "ctx"),
        P("fsdp"),
        P(),
        P(),
        P("fsdp", None),
        P(),
        P("fsdp", None),
        P(),
        P(),
        P(),
        P("fsdp", None),
        P(),
        P("fsdp", None),
        P(),
        P("fsdp", "ctx", None),
    )
    out_specs = (
        P("fsdp", "ctx", None),
        P("fsdp", "ctx", None),
        P(),
        P(),
        P("fsdp", None),
        P(),
        P("fsdp", None),
        P(),
        P(),
        P(),
        P("fsdp", None),
        P(),
        P("fsdp", None),
        P(),
    )

    def body(*args):
        return per_device(parts, spans, *args)

    return jax.shard_map(body, mesh=mesh, in_specs=in_specs, out_specs=out_specs, check_vma=False)
```

```python
import jax
import jax.numpy as jnp
from jax import lax
from jax.sharding import PartitionSpec as P

HEAD_DIM = 64
EPSILON = 1e-05
NEGATIVE = -1e30
LOW = 64


def layer_norm(values, gain, bias):
    center = values - jnp.mean(values, axis=-1, keepdims=True)
    inverse = lax.rsqrt(jnp.mean(center * center, axis=-1, keepdims=True) + EPSILON)
    normed = center * inverse
    return (normed * gain + bias, normed, inverse)


def norm_back(upper, normed, inverse, gain):
    scaled = upper * gain
    return inverse * (
        scaled
        - jnp.mean(scaled, axis=-1, keepdims=True)
        - normed * jnp.mean(scaled * normed, axis=-1, keepdims=True)
    )


def gelu(values):
    return jax.nn.gelu(values, approximate=True)


def term_of(left, right):
    return jnp.einsum("ti,tj->ij", left, right, preferred_element_type=jnp.float32)


def gate(values, *milestones):
    return lax.optimization_barrier((*values, *milestones))[: len(values)]


def swap(value, axis, size, step):
    return lax.ppermute(value, axis, [(i, i ^ step) for i in range(size)])


def middle(columns):
    return max(columns // 2 // 128, 1) * 128


def near_rows(local):
    return swap(local, "fsdp", 4, 1), swap(local, "fsdp", 4, 2)


def far_rows(along_x, along_y):
    split = middle(along_x.shape[1])
    return swap(along_x[:, :split], "fsdp", 4, 2), swap(along_y[:, split:], "fsdp", 4, 1)


def own_half(shard):
    half = shard.shape[0] // 2
    return lax.dynamic_slice_in_dim(shard, (lax.axis_index("ctx") % 2) * half, half, 0)


def assemble(shard, near, far):
    rows, columns = shard.shape
    half = rows // 2
    place = lax.axis_index("fsdp")
    core = lax.axis_index("ctx") % 2
    full = jnp.zeros((4 * rows, columns), shard.dtype)
    full = lax.dynamic_update_slice(full, shard, (place * rows, 0))
    mine = ((near[0], 1, 0), (near[1], 2, 0), (far[0], 3, 0), (far[1], 3, middle(columns)))
    others = [swap(piece, "ctx", 8, 1) for piece, _, _ in mine]
    for piece, step, column in mine:
        full = lax.dynamic_update_slice(full, piece, ((place ^ step) * rows + core * half, column))
    for other, (_, step, column) in zip(others, mine):
        start = (place ^ step) * rows + (1 - core) * half
        full = lax.dynamic_update_slice(full, other, (start, column))
    return full


def stacked(local, near, far):
    return jnp.concatenate([local, *near, jnp.concatenate(far, axis=1)], axis=0)


def placed(bit, mine, other, axis):
    first = jnp.where(bit == 0, mine, other)
    second = jnp.where(bit == 0, other, mine)
    return jnp.concatenate([first, second], axis=axis)


def level_bits():
    number = lax.axis_index("ctx")
    return number % 2, (number // 2) % 2, number // 4


def core_sum(part):
    core = level_bits()[0]
    half = part.shape[0] // 2
    sent = lax.dynamic_slice_in_dim(part, (1 - core) * half, half, 0).astype(jnp.bfloat16)
    kept = lax.dynamic_slice_in_dim(part, core * half, half, 0)
    return kept + swap(sent, "ctx", 8, 1).astype(jnp.float32)


def fold(kept, bit, step, axis):
    width = kept.shape[axis] // 2
    sent = lax.dynamic_slice_in_dim(kept, (1 - bit) * width, width, axis).astype(jnp.bfloat16)
    mine = lax.dynamic_slice_in_dim(kept, bit * width, width, axis)
    return mine + swap(sent, "ctx", 8, step).astype(jnp.float32)


def ctx_sum(total, columns, axis, gates):
    core, low, high = level_bits()
    (total,) = gate((total,), *gates[0])
    total = fold(total, low, 2, axis)
    (total,) = gate((total,), *gates[1])
    total = fold(total, high, 4, axis)
    (total,) = gate((total.astype(jnp.bfloat16),), *gates[2])
    total = placed(high, total, swap(total, "ctx", 8, 4), axis)
    (total,) = gate((total,), *gates[3])
    total = placed(low, total, swap(total, "ctx", 8, 2), axis)
    (total,) = gate((total,), *gates[4])
    total = placed(core, total, swap(total, "ctx", 8, 1), 0)
    return total[:, :columns].astype(jnp.float32)


def all_sum(values, fast):
    if not fast:
        return lax.psum(values, ("fsdp", "ctx"))
    shape = values.shape
    values = values.reshape(-1, 128)
    values = values + swap(values, "ctx", 8, 1)
    for axis, size, unit in (("fsdp", 4, 1), ("ctx", 8, 2)):
        one, two, three = (swap(values, axis, size, step * unit) for step in (1, 2, 3))
        values = (values + one) + (two + three)
    return values.reshape(shape)


def per_device(
    parts,
    spans,
    block_input,
    positions,
    prefix,
    first_gain,
    first_bias,
    query_key_value,
    query_value_bias,
    output_weight,
    output_bias,
    second_gain,
    second_bias,
    expand_weight,
    expand_bias,
    contract_weight,
    contract_bias,
    cotangent,
):
    fast = parts == 4 and spans == 8
    sequences, piece, width = block_input.shape
    hidden = expand_weight.shape[1]
    heads = width // HEAD_DIM
    scale = HEAD_DIM ** (-0.5)
    rows = sequences * piece
    length = spans * piece
    slots = -(-sequences * heads // spans)
    band = slots * HEAD_DIM
    number = lax.axis_index("ctx")

    if fast:
        joint_near = near_rows(own_half(query_key_value))
        joint_far = far_rows(*joint_near)
        joint_full = assemble(query_key_value, joint_near, joint_far)
        output_half, expand_half, contract_half = gate(
            (own_half(output_weight), own_half(expand_weight), own_half(contract_weight)),
            *joint_far,
        )
        output_near = near_rows(output_half)
        expand_near = near_rows(expand_half)
    else:
        joint_full, output_full, expand_full, contract_full = (
            lax.all_gather(w, "fsdp", axis=0, tiled=True)
            for w in (query_key_value, output_weight, expand_weight, contract_weight)
        )

    def to_bands(tensors):
        wide = []
        for tensor in tensors:
            flat = [tensor[s * piece : (s + 1) * piece] for s in range(sequences)]
            flat.append(jnp.zeros((piece, spans * band - sequences * width), tensor.dtype))
            wide.append(jnp.concatenate(flat, axis=1))
        blocks = [
            jnp.concatenate([w[:, j * band : (j + 1) * band] for w in wide], axis=1)
            for j in range(spans)
        ]
        return jnp.stack(blocks)

    def from_bands(blocks, count):
        whole = []
        for t in range(count):
            flat = jnp.concatenate(
                [blocks[j, :, t * band : (t + 1) * band] for j in range(spans)], axis=1
            )
            whole.append(
                jnp.concatenate(
                    [flat[:, s * width : (s + 1) * width] for s in range(sequences)], axis=0
                )
            )
        return jnp.concatenate(whole, axis=1)

    def exchange(blocks):
        return lax.all_to_all(blocks, "ctx", 0, 0, tiled=True)

    def heads_of(flat, number_of):
        starts = [number_of * band + i * HEAD_DIM for i in range(slots)]
        return jnp.stack([flat[:, start : start + HEAD_DIM] for start in starts])

    input_rows = block_input.reshape(rows, width).astype(jnp.float32)
    first_out, first_normed, first_inverse = layer_norm(input_rows, first_gain, first_bias)
    first_round = first_out.astype(jnp.bfloat16)
    joint = jnp.dot(first_round, joint_full, preferred_element_type=jnp.float32)
    query = (joint[:, :width] + query_value_bias[0]).astype(jnp.bfloat16)
    keys = joint[:, width : 2 * width].astype(jnp.bfloat16)
    values = (joint[:, 2 * width :] + query_value_bias[1]).astype(jnp.bfloat16)
    digits = jnp.concatenate([positions // LOW, positions % LOW], axis=0).T.astype(jnp.bfloat16)
    digits = jnp.broadcast_to(digits[None], (spans, piece, 2 * sequences))
    payload = jnp.concatenate([to_bands((query, keys, values)), digits], axis=2)
    if fast:
        output_near = gate(output_near, payload)
        expand_near = gate(expand_near, payload)
        output_far = far_rows(*output_near)
        expand_far = far_rows(*expand_near)
        contract_near = near_rows(gate((contract_half,), *expand_near)[0])
    received = exchange(payload)
    received = received.reshape(length, 3 * band + 2 * sequences)
    query_heads, key_heads, value_heads = (heads_of(received, t) for t in range(3))
    digits = received[:, 3 * band :].astype(jnp.int32)
    places = digits[:, :sequences].T * LOW + digits[:, sequences:].T
    limits = jnp.maximum(places, prefix[:, None] - 1)
    owner = jnp.minimum((number * slots + jnp.arange(slots)) // heads, sequences - 1)

    def of_owner(table):
        chosen = jnp.broadcast_to(table[0][None], (slots, length))
        for row in range(1, sequences):
            chosen = jnp.where(owner[:, None] == row, table[row][None], chosen)
        return chosen

    visible = of_owner(places)[:, None, :] <= of_owner(limits)[:, :, None]
    scores = (
        jnp.einsum("pqd,pkd->pqk", query_heads, key_heads, preferred_element_type=jnp.float32)
        * scale
    )
    scores = jnp.where(visible, scores, NEGATIVE)
    top = jnp.max(scores, axis=-1, keepdims=True)
    log_total = top + jnp.log(jnp.sum(jnp.exp(scores - top), axis=-1, keepdims=True))
    chance = jnp.exp(scores - log_total)
    shares = chance.astype(jnp.bfloat16)
    mixed_heads = jnp.einsum(
        "pqk,pkd->pqd", shares, value_heads, preferred_element_type=jnp.float32
    ).astype(jnp.bfloat16)

    def to_pieces(tensor):
        return jnp.concatenate([tensor[i] for i in range(slots)], axis=1).reshape(
            spans, piece, band
        )

    mixed_pieces = to_pieces(mixed_heads)
    upper = cotangent.reshape(rows, width)
    if fast:
        output_far = gate(output_far, mixed_pieces)
        expand_far = gate(expand_far, mixed_pieces)
        contract_near = gate(contract_near, mixed_pieces)
        output_full = assemble(output_weight, output_near, output_far)
        expand_full = assemble(expand_weight, expand_near, expand_far)
        contract_far = far_rows(*contract_near)
        upper_near = near_rows(gate((upper,), *contract_near)[0])
    mixed = from_bands(exchange(mixed_pieces), 1)
    residual = (
        input_rows + jnp.dot(mixed, output_full, preferred_element_type=jnp.float32) + output_bias
    )
    second_out, second_normed, second_inverse = layer_norm(residual, second_gain, second_bias)
    second_round = second_out.astype(jnp.bfloat16)
    if fast:
        contract_far = gate(contract_far, second_round)
        contract_full = assemble(contract_weight, contract_near, contract_far)
        upper_near = gate(upper_near, second_round)
        upper_far = far_rows(*upper_near)
    before = jnp.dot(second_round, expand_full, preferred_element_type=jnp.float32) + expand_bias
    activated, gelu_back = jax.vjp(gelu, before)
    after_round = activated.astype(jnp.bfloat16)
    block_output = (
        (
            residual
            + jnp.dot(after_round, contract_full, preferred_element_type=jnp.float32)
            + contract_bias
        )
        .astype(jnp.bfloat16)
        .reshape(sequences, piece, width)
    )
    upper_wide = upper.astype(jnp.float32)
    after_grad = jnp.dot(upper, contract_full.T, preferred_element_type=jnp.float32)
    before_grad = gelu_back(after_grad)[0]
    before_round = before_grad.astype(jnp.bfloat16)
    second_grad = jnp.dot(before_round, expand_full.T, preferred_element_type=jnp.float32)
    residual_grad = upper_wide + norm_back(second_grad, second_normed, second_inverse, second_gain)
    residual_round = residual_grad.astype(jnp.bfloat16)
    mixed_grad = jnp.dot(residual_round, output_full.T, preferred_element_type=jnp.float32).astype(
        jnp.bfloat16
    )

    mixed_payload = to_bands((mixed_grad,))
    if fast:
        place = lax.axis_index("fsdp")
        narrow = width // parts
        broad = hidden // parts
        lefts = jnp.stack(
            [
                jnp.concatenate(
                    [
                        after_round[:, p * broad : (p + 1) * broad],
                        first_round[:, p * narrow : (p + 1) * narrow],
                        mixed[:, p * narrow : (p + 1) * narrow],
                        second_round[:, p * narrow : (p + 1) * narrow],
                    ],
                    axis=1,
                )
                for p in range(parts)
            ]
        )
        picked = [lax.dynamic_index_in_dim(lefts, place ^ s, 0, False) for s in range(4)]
        moved = [swap(picked[s], "fsdp", 4, s) for s in (1, 2, 3)]
        before_near = near_rows(before_round)
        residual_near = near_rows(residual_round)
        before_near = gate(before_near, mixed_payload)
        residual_near = gate(residual_near, mixed_payload)
        moved = gate(moved, mixed_payload)
        before_far = far_rows(*before_near)
        residual_far = far_rows(*residual_near)
        left = jnp.concatenate([picked[0], *moved], axis=0)
        after_left = left[:, :broad]
        first_left = left[:, broad : broad + narrow]
        mixed_left = left[:, broad + narrow : broad + 2 * narrow]
        second_left = left[:, broad + 2 * narrow :]
    above = heads_of(exchange(mixed_payload).reshape(length, band), 0)
    flows = jnp.sum(
        above.astype(jnp.float32) * mixed_heads.astype(jnp.float32), axis=-1, keepdims=True
    )
    share_grad = jnp.einsum("pqd,pkd->pqk", above, value_heads, preferred_element_type=jnp.float32)
    score_round = (chance * (share_grad - flows)).astype(jnp.bfloat16)
    query_grad = (
        jnp.einsum("pqk,pkd->pqd", score_round, key_heads, preferred_element_type=jnp.float32)
        * scale
    )
    key_grad = (
        jnp.einsum("pqk,pqd->pkd", score_round, query_heads, preferred_element_type=jnp.float32)
        * scale
    )
    value_grad = jnp.einsum("pqk,pqd->pkd", shares, above, preferred_element_type=jnp.float32)
    pieces = [to_pieces(g.astype(jnp.bfloat16)) for g in (query_grad, key_grad, value_grad)]
    joint_payload = jnp.concatenate(pieces, axis=2)
    joint_grad = from_bands(exchange(joint_payload), 3)

    def bias_sum(grad):
        line = jnp.zeros((spans * band,), jnp.float32)
        line = lax.dynamic_update_slice(line, jnp.sum(grad, axis=1).reshape(band), (number * band,))
        return jnp.sum(line[: sequences * width].reshape(sequences, width), axis=0)

    joint_later = joint_grad
    if fast:
        joint_near = near_rows(joint_grad)
        joint_far = far_rows(*joint_near)

        def core_of(rows_left, right):
            right = jnp.pad(right, ((0, 0), (0, -right.shape[1] % 512)))
            return core_sum(term_of(rows_left, right))

        joint_core = core_of(first_left, stacked(joint_grad, joint_near, joint_far))
        (joint_later,) = gate((joint_grad,), joint_core)
    first_grad = jnp.dot(joint_later, joint_full.T, preferred_element_type=jnp.float32)
    input_gradient = (
        residual_grad + norm_back(first_grad, first_normed, first_inverse, first_gain)
    ).reshape(sequences, piece, width)

    if fast:
        contract_sum = ctx_sum(
            core_sum(term_of(after_left, stacked(upper, upper_near, upper_far))),
            width,
            0,
            ((above,), (score_round,), (joint_grad,), joint_near, joint_far),
        )
        before_far = gate(before_far, joint_grad)
        residual_far = gate(residual_far, joint_payload)
        side = ((joint_grad,), joint_near, joint_far, (), ())
        expand_core = core_of(second_left, stacked(before_round, before_near, before_far))
        expand_sum = ctx_sum(expand_core, hidden, 1, side)
        output_core = core_of(mixed_left, stacked(residual_round, residual_near, residual_far))
        output_sum = ctx_sum(output_core, width, 1, side)
        joint_sum = ctx_sum(joint_core, 3 * width, 1, ((),) * 5)
    else:
        joint_sum, output_sum, expand_sum, contract_sum = (
            lax.psum(
                lax.psum_scatter(term_of(x, y), "fsdp", scatter_dimension=0, tiled=True), "ctx"
            )
            for x, y in (
                (first_round, joint_grad),
                (mixed, residual_round),
                (second_round, before_round),
                (after_round, upper),
            )
        )
    small = all_sum(
        jnp.concatenate(
            [
                jnp.sum(residual_grad, axis=0),
                jnp.sum(second_grad * second_normed, axis=0),
                jnp.sum(second_grad, axis=0),
                jnp.sum(upper_wide, axis=0),
                jnp.sum(before_grad, axis=0),
                jnp.sum(first_grad * first_normed, axis=0),
                jnp.sum(first_grad, axis=0),
                bias_sum(query_grad),
                bias_sum(value_grad),
            ]
        ),
        fast,
    )
    early, late = small[: 4 * width + hidden], small[4 * width + hidden :]
    return (
        block_output,
        input_gradient,
        late[:width],
        late[width : 2 * width],
        joint_sum,
        late[2 * width :].reshape(2, width),
        output_sum,
        early[:width],
        early[width : 2 * width],
        early[2 * width : 3 * width],
        expand_sum,
        early[4 * width :],
        contract_sum,
        early[3 * width : 4 * width],
    )


def solution(mesh):
    parts, spans = mesh.shape["fsdp"], mesh.shape["ctx"]
    in_specs = (
        P("fsdp", "ctx", None),
        P("fsdp", "ctx"),
        P("fsdp"),
        P(),
        P(),
        P("fsdp", None),
        P(),
        P("fsdp", None),
        P(),
        P(),
        P(),
        P("fsdp", None),
        P(),
        P("fsdp", None),
        P(),
        P("fsdp", "ctx", None),
    )
    out_specs = (
        P("fsdp", "ctx", None),
        P("fsdp", "ctx", None),
        P(),
        P(),
        P("fsdp", None),
        P(),
        P("fsdp", None),
        P(),
        P(),
        P(),
        P("fsdp", None),
        P(),
        P("fsdp", None),
        P(),
    )

    def body(*args):
        return per_device(parts, spans, *args)

    return jax.shard_map(body, mesh=mesh, in_specs=in_specs, out_specs=out_specs, check_vma=False)
```

```python
import jax
import jax.numpy as jnp
from jax import lax
from jax.sharding import PartitionSpec as P

HEAD_DIM = 64
EPSILON = 1e-05
NEGATIVE = -1e30
LOW = 64


def layer_norm(values, gain, bias):
    center = values - jnp.mean(values, axis=-1, keepdims=True)
    inverse = lax.rsqrt(jnp.mean(center * center, axis=-1, keepdims=True) + EPSILON)
    normed = center * inverse
    return (normed * gain + bias, normed, inverse)


def norm_back(upper, normed, inverse, gain):
    scaled = upper * gain
    return inverse * (
        scaled
        - jnp.mean(scaled, axis=-1, keepdims=True)
        - normed * jnp.mean(scaled * normed, axis=-1, keepdims=True)
    )


def gelu(values):
    return jax.nn.gelu(values, approximate=True)


def term_of(left, right):
    return jnp.einsum("ti,tj->ij", left, right, preferred_element_type=jnp.float32)


def gate(values, *milestones):
    return lax.optimization_barrier((*values, *milestones))[: len(values)]


def swap(value, axis, size, step):
    return lax.ppermute(value, axis, [(i, i ^ step) for i in range(size)])


def middle(columns):
    return max(columns // 2 // 128, 1) * 128


def near_rows(local):
    return swap(local, "fsdp", 4, 1), swap(local, "fsdp", 4, 2)


def far_rows(along_x, along_y):
    split = middle(along_x.shape[1])
    return swap(along_x[:, :split], "fsdp", 4, 2), swap(along_y[:, split:], "fsdp", 4, 1)


def own_half(shard):
    half = shard.shape[0] // 2
    return lax.dynamic_slice_in_dim(shard, (lax.axis_index("ctx") % 2) * half, half, 0)


def assemble(shard, near, far):
    rows, columns = shard.shape
    half = rows // 2
    place = lax.axis_index("fsdp")
    core = lax.axis_index("ctx") % 2
    full = jnp.zeros((4 * rows, columns), shard.dtype)
    full = lax.dynamic_update_slice(full, shard, (place * rows, 0))
    mine = ((near[0], 1, 0), (near[1], 2, 0), (far[0], 3, 0), (far[1], 3, middle(columns)))
    others = [swap(piece, "ctx", 8, 1) for piece, _, _ in mine]
    for piece, step, column in mine:
        full = lax.dynamic_update_slice(full, piece, ((place ^ step) * rows + core * half, column))
    for other, (_, step, column) in zip(others, mine):
        start = (place ^ step) * rows + (1 - core) * half
        full = lax.dynamic_update_slice(full, other, (start, column))
    return full


def stacked(local, near, far):
    return jnp.concatenate([local, *near, jnp.concatenate(far, axis=1)], axis=0)


def placed(bit, mine, other, axis):
    first = jnp.where(bit == 0, mine, other)
    second = jnp.where(bit == 0, other, mine)
    return jnp.concatenate([first, second], axis=axis)


def level_bits():
    number = lax.axis_index("ctx")
    return number % 2, (number // 2) % 2, number // 4


def core_sum(part):
    core = level_bits()[0]
    half = part.shape[0] // 2
    sent = lax.dynamic_slice_in_dim(part, (1 - core) * half, half, 0).astype(jnp.bfloat16)
    kept = lax.dynamic_slice_in_dim(part, core * half, half, 0)
    return kept + swap(sent, "ctx", 8, 1).astype(jnp.float32)


def fold(kept, bit, step, axis):
    width = kept.shape[axis] // 2
    sent = lax.dynamic_slice_in_dim(kept, (1 - bit) * width, width, axis).astype(jnp.bfloat16)
    mine = lax.dynamic_slice_in_dim(kept, bit * width, width, axis)
    return mine + swap(sent, "ctx", 8, step).astype(jnp.float32)


def ctx_sum(total, columns, axis, gates):
    core, low, high = level_bits()
    (total,) = gate((total,), *gates[0])
    total = fold(total, low, 2, axis)
    (total,) = gate((total,), *gates[1])
    total = fold(total, high, 4, axis)
    (total,) = gate((total.astype(jnp.bfloat16),), *gates[2])
    total = placed(high, total, swap(total, "ctx", 8, 4), axis)
    (total,) = gate((total,), *gates[3])
    total = placed(low, total, swap(total, "ctx", 8, 2), axis)
    (total,) = gate((total,), *gates[4])
    total = placed(core, total, swap(total, "ctx", 8, 1), 0)
    return total[:, :columns].astype(jnp.float32)


def all_sum(values, fast):
    if not fast:
        return lax.psum(values, ("fsdp", "ctx"))
    shape = values.shape
    values = values.reshape(-1, 128)
    values = values + swap(values, "ctx", 8, 1)
    for axis, size, unit in (("fsdp", 4, 1), ("ctx", 8, 2)):
        one, two, three = (swap(values, axis, size, step * unit) for step in (1, 2, 3))
        values = (values + one) + (two + three)
    return values.reshape(shape)


def per_device(
    parts,
    spans,
    block_input,
    positions,
    prefix,
    first_gain,
    first_bias,
    query_key_value,
    query_value_bias,
    output_weight,
    output_bias,
    second_gain,
    second_bias,
    expand_weight,
    expand_bias,
    contract_weight,
    contract_bias,
    cotangent,
):
    fast = parts == 4 and spans == 8
    sequences, piece, width = block_input.shape
    hidden = expand_weight.shape[1]
    heads = width // HEAD_DIM
    scale = HEAD_DIM ** (-0.5)
    rows = sequences * piece
    length = spans * piece
    slots = -(-sequences * heads // spans)
    band = slots * HEAD_DIM
    number = lax.axis_index("ctx")

    if fast:
        joint_near = near_rows(own_half(query_key_value))
        joint_far = far_rows(*joint_near)
        joint_full = assemble(query_key_value, joint_near, joint_far)
        output_half, expand_half, contract_half = gate(
            (own_half(output_weight), own_half(expand_weight), own_half(contract_weight)),
            *joint_far,
        )
        output_near = near_rows(output_half)
        expand_near = near_rows(expand_half)
    else:
        joint_full, output_full, expand_full, contract_full = (
            lax.all_gather(w, "fsdp", axis=0, tiled=True)
            for w in (query_key_value, output_weight, expand_weight, contract_weight)
        )

    def to_bands(tensors):
        wide = []
        for tensor in tensors:
            flat = [tensor[s * piece : (s + 1) * piece] for s in range(sequences)]
            flat.append(jnp.zeros((piece, spans * band - sequences * width), tensor.dtype))
            wide.append(jnp.concatenate(flat, axis=1))
        blocks = [
            jnp.concatenate([w[:, j * band : (j + 1) * band] for w in wide], axis=1)
            for j in range(spans)
        ]
        return jnp.stack(blocks)

    def from_bands(blocks, count):
        whole = []
        for t in range(count):
            flat = jnp.concatenate(
                [blocks[j, :, t * band : (t + 1) * band] for j in range(spans)], axis=1
            )
            whole.append(
                jnp.concatenate(
                    [flat[:, s * width : (s + 1) * width] for s in range(sequences)], axis=0
                )
            )
        return jnp.concatenate(whole, axis=1)

    def exchange(blocks):
        return lax.all_to_all(blocks, "ctx", 0, 0, tiled=True)

    def heads_of(flat, number_of):
        starts = [number_of * band + i * HEAD_DIM for i in range(slots)]
        return jnp.stack([flat[:, start : start + HEAD_DIM] for start in starts])

    input_rows = block_input.reshape(rows, width).astype(jnp.float32)
    first_out, first_normed, first_inverse = layer_norm(input_rows, first_gain, first_bias)
    first_round = first_out.astype(jnp.bfloat16)
    joint = jnp.dot(first_round, joint_full, preferred_element_type=jnp.float32)
    query = (joint[:, :width] + query_value_bias[0]).astype(jnp.bfloat16)
    keys = joint[:, width : 2 * width].astype(jnp.bfloat16)
    values = (joint[:, 2 * width :] + query_value_bias[1]).astype(jnp.bfloat16)
    digits = jnp.concatenate([positions // LOW, positions % LOW], axis=0).T.astype(jnp.bfloat16)
    digits = jnp.broadcast_to(digits[None], (spans, piece, 2 * sequences))
    payload = jnp.concatenate([to_bands((query, keys, values)), digits], axis=2)
    if fast:
        output_near = gate(output_near, payload)
        expand_near = gate(expand_near, payload)
        output_far = far_rows(*output_near)
        expand_far = far_rows(*expand_near)
        contract_near = near_rows(gate((contract_half,), *expand_near)[0])
    received = exchange(payload)
    received = received.reshape(length, 3 * band + 2 * sequences)
    query_heads, key_heads, value_heads = (heads_of(received, t) for t in range(3))
    digits = received[:, 3 * band :].astype(jnp.int32)
    places = digits[:, :sequences].T * LOW + digits[:, sequences:].T
    limits = jnp.maximum(places, prefix[:, None] - 1)
    owner = jnp.minimum((number * slots + jnp.arange(slots)) // heads, sequences - 1)

    def of_owner(table):
        chosen = jnp.broadcast_to(table[0][None], (slots, length))
        for row in range(1, sequences):
            chosen = jnp.where(owner[:, None] == row, table[row][None], chosen)
        return chosen

    visible = of_owner(places)[:, None, :] <= of_owner(limits)[:, :, None]
    scores = (
        jnp.einsum("pqd,pkd->pqk", query_heads, key_heads, preferred_element_type=jnp.float32)
        * scale
    )
    scores = jnp.where(visible, scores, NEGATIVE)
    top = jnp.max(scores, axis=-1, keepdims=True)
    log_total = top + jnp.log(jnp.sum(jnp.exp(scores - top), axis=-1, keepdims=True))
    chance = jnp.exp(scores - log_total)
    shares = chance.astype(jnp.bfloat16)
    mixed_heads = jnp.einsum(
        "pqk,pkd->pqd", shares, value_heads, preferred_element_type=jnp.float32
    ).astype(jnp.bfloat16)

    def to_pieces(tensor):
        return jnp.concatenate([tensor[i] for i in range(slots)], axis=1).reshape(
            spans, piece, band
        )

    mixed_pieces = to_pieces(mixed_heads)
    upper = cotangent.reshape(rows, width)
    if fast:
        output_far = gate(output_far, mixed_pieces)
        expand_far = gate(expand_far, mixed_pieces)
        contract_near = gate(contract_near, mixed_pieces)
        output_full = assemble(output_weight, output_near, output_far)
        expand_full = assemble(expand_weight, expand_near, expand_far)
        contract_far = far_rows(*contract_near)
        upper_near = near_rows(gate((upper,), *contract_near)[0])
    mixed = from_bands(exchange(mixed_pieces), 1)
    residual = (
        input_rows + jnp.dot(mixed, output_full, preferred_element_type=jnp.float32) + output_bias
    )
    second_out, second_normed, second_inverse = layer_norm(residual, second_gain, second_bias)
    second_round = second_out.astype(jnp.bfloat16)
    if fast:
        contract_far = gate(contract_far, second_round)
        contract_full = assemble(contract_weight, contract_near, contract_far)
        upper_near = gate(upper_near, second_round)
        upper_far = far_rows(*upper_near)
    before = jnp.dot(second_round, expand_full, preferred_element_type=jnp.float32) + expand_bias
    activated, gelu_back = jax.vjp(gelu, before)
    after_round = activated.astype(jnp.bfloat16)
    block_output = (
        (
            residual
            + jnp.dot(after_round, contract_full, preferred_element_type=jnp.float32)
            + contract_bias
        )
        .astype(jnp.bfloat16)
        .reshape(sequences, piece, width)
    )
    upper_wide = upper.astype(jnp.float32)
    after_grad = jnp.dot(upper, contract_full.T, preferred_element_type=jnp.float32)
    before_grad = gelu_back(after_grad)[0]
    before_round = before_grad.astype(jnp.bfloat16)
    second_grad = jnp.dot(before_round, expand_full.T, preferred_element_type=jnp.float32)
    residual_grad = upper_wide + norm_back(second_grad, second_normed, second_inverse, second_gain)
    residual_round = residual_grad.astype(jnp.bfloat16)
    mixed_grad = jnp.dot(residual_round, output_full.T, preferred_element_type=jnp.float32).astype(
        jnp.bfloat16
    )

    mixed_payload = to_bands((mixed_grad,))
    if fast:
        place = lax.axis_index("fsdp")
        narrow = width // parts
        broad = hidden // parts
        lefts = jnp.stack(
            [
                jnp.concatenate(
                    [
                        after_round[:, p * broad : (p + 1) * broad],
                        first_round[:, p * narrow : (p + 1) * narrow],
                        mixed[:, p * narrow : (p + 1) * narrow],
                        second_round[:, p * narrow : (p + 1) * narrow],
                    ],
                    axis=1,
                )
                for p in range(parts)
            ]
        )
        picked = [lax.dynamic_index_in_dim(lefts, place ^ s, 0, False) for s in range(4)]
        moved = [swap(picked[s], "fsdp", 4, s) for s in (1, 2, 3)]
        before_near = near_rows(before_round)
        residual_near = near_rows(residual_round)
        before_near = gate(before_near, mixed_payload)
        residual_near = gate(residual_near, mixed_payload)
        moved = gate(moved, mixed_payload)
        before_far = far_rows(*before_near)
        residual_far = far_rows(*residual_near)
        left = jnp.concatenate([picked[0], *moved], axis=0)
        after_left = left[:, :broad]
        first_left = left[:, broad : broad + narrow]
        mixed_left = left[:, broad + narrow : broad + 2 * narrow]
        second_left = left[:, broad + 2 * narrow :]
    above = heads_of(exchange(mixed_payload).reshape(length, band), 0)
    flows = jnp.sum(
        above.astype(jnp.float32) * mixed_heads.astype(jnp.float32), axis=-1, keepdims=True
    )
    share_grad = jnp.einsum("pqd,pkd->pqk", above, value_heads, preferred_element_type=jnp.float32)
    score_round = (chance * (share_grad - flows)).astype(jnp.bfloat16)
    query_grad = (
        jnp.einsum("pqk,pkd->pqd", score_round, key_heads, preferred_element_type=jnp.float32)
        * scale
    )
    key_grad = (
        jnp.einsum("pqk,pqd->pkd", score_round, query_heads, preferred_element_type=jnp.float32)
        * scale
    )
    value_grad = jnp.einsum("pqk,pqd->pkd", shares, above, preferred_element_type=jnp.float32)
    pieces = [to_pieces(g.astype(jnp.bfloat16)) for g in (query_grad, key_grad, value_grad)]
    joint_payload = jnp.concatenate(pieces, axis=2)
    joint_grad = from_bands(exchange(joint_payload), 3)

    def bias_sum(grad):
        line = jnp.zeros((spans * band,), jnp.float32)
        line = lax.dynamic_update_slice(line, jnp.sum(grad, axis=1).reshape(band), (number * band,))
        return jnp.sum(line[: sequences * width].reshape(sequences, width), axis=0)

    joint_later = joint_grad
    if fast:
        joint_near = near_rows(joint_grad)
        joint_far = far_rows(*joint_near)

        def core_of(rows_left, right):
            right = jnp.pad(right, ((0, 0), (0, -right.shape[1] % 512)))
            return core_sum(term_of(rows_left, right))

        joint_core = core_of(first_left, stacked(joint_grad, joint_near, joint_far))
        (joint_later,) = gate((joint_grad,), joint_core)
    first_grad = jnp.dot(joint_later, joint_full.T, preferred_element_type=jnp.float32)
    input_gradient = (
        residual_grad + norm_back(first_grad, first_normed, first_inverse, first_gain)
    ).reshape(sequences, piece, width)

    if fast:
        contract_sum = ctx_sum(
            core_sum(term_of(after_left, stacked(upper, upper_near, upper_far))),
            width,
            0,
            ((above,), (score_round,), (joint_grad,), joint_near, joint_far),
        )
        before_far = gate(before_far, joint_payload)
        residual_far = gate(residual_far, joint_payload)
        side = ((joint_grad,), joint_near, joint_far, (), ())
        expand_core = core_of(second_left, stacked(before_round, before_near, before_far))
        expand_sum = ctx_sum(expand_core, hidden, 1, side)
        output_core = core_of(mixed_left, stacked(residual_round, residual_near, residual_far))
        output_sum = ctx_sum(output_core, width, 1, side)
        joint_sum = ctx_sum(joint_core, 3 * width, 1, ((),) * 5)
    else:
        joint_sum, output_sum, expand_sum, contract_sum = (
            lax.psum(
                lax.psum_scatter(term_of(x, y), "fsdp", scatter_dimension=0, tiled=True), "ctx"
            )
            for x, y in (
                (first_round, joint_grad),
                (mixed, residual_round),
                (second_round, before_round),
                (after_round, upper),
            )
        )
    small = all_sum(
        jnp.concatenate(
            [
                jnp.sum(residual_grad, axis=0),
                jnp.sum(second_grad * second_normed, axis=0),
                jnp.sum(second_grad, axis=0),
                jnp.sum(upper_wide, axis=0),
                jnp.sum(before_grad, axis=0),
                jnp.sum(first_grad * first_normed, axis=0),
                jnp.sum(first_grad, axis=0),
                bias_sum(query_grad),
                bias_sum(value_grad),
            ]
        ),
        fast,
    )
    early, late = small[: 4 * width + hidden], small[4 * width + hidden :]
    return (
        block_output,
        input_gradient,
        late[:width],
        late[width : 2 * width],
        joint_sum,
        late[2 * width :].reshape(2, width),
        output_sum,
        early[:width],
        early[width : 2 * width],
        early[2 * width : 3 * width],
        expand_sum,
        early[4 * width :],
        contract_sum,
        early[3 * width : 4 * width],
    )


def solution(mesh):
    parts, spans = mesh.shape["fsdp"], mesh.shape["ctx"]
    in_specs = (
        P("fsdp", "ctx", None),
        P("fsdp", "ctx"),
        P("fsdp"),
        P(),
        P(),
        P("fsdp", None),
        P(),
        P("fsdp", None),
        P(),
        P(),
        P(),
        P("fsdp", None),
        P(),
        P("fsdp", None),
        P(),
        P("fsdp", "ctx", None),
    )
    out_specs = (
        P("fsdp", "ctx", None),
        P("fsdp", "ctx", None),
        P(),
        P(),
        P("fsdp", None),
        P(),
        P("fsdp", None),
        P(),
        P(),
        P(),
        P("fsdp", None),
        P(),
        P("fsdp", None),
        P(),
    )

    def body(*args):
        return per_device(parts, spans, *args)

    return jax.shard_map(body, mesh=mesh, in_specs=in_specs, out_specs=out_specs, check_vma=False)
```
